32 devices in a mesh: ctx: 16 (over z, y, x), head: 2 (over core).
Axes of the slice: x: 2, y: 2, z: 4, core: 2. Of those that a mesh axis runs over, the one named last changes fastest.
Arguments:
- q_home: bfloat16 [8192, 2048], P('ctx', 'head'), may hold values from -18 to 18
- k_home: bfloat16 [8192, 512], P('ctx', 'head'), may hold values from -6 to 6
- value_slots_local: bfloat16 [8192, 512], P('ctx', 'head'), may hold values from -16 to 16
- out_weight: bfloat16 [2048, 4096], P('head'), may hold values from -0.125 to 0.125
- router: float32 [8192], P('ctx'), may hold values from 0.25 to 1
- positions: int32 [8192], P('ctx'), may hold values from 0 to 32767, as said below
- counts: int32 [16], P('ctx'), may hold values from 1 to 512, 2048 in all
Outputs:
- routed_update: bfloat16 [8192, 4096], P('ctx', 'head')
The draws below stay inside these ranges and needn't reach their ends.
Inputs may be any that keep to these rules, and one draw needn't show every extreme that they name: counts sum to 2048; the busiest shard holds exactly 512. The 512 positions of shard d are distinct, increasing, and lie in [d * 2048, (d + 1) * 2048).
All inputs are finite; a program needn't handle non-finite values.
Results may differ from the reference program's by a relative error of at most 0.033.
Values may be sent and summed in bfloat16 or wider, within the bound.
A program may use at most 128 MiB of HBM per device.

```python
import math
import jax
import jax.numpy as jnp
import numpy as np
from jax import lax

D = 4096
QUERY_HEADS = 16
KEY_VALUE_HEADS = 4
HEAD_WIDTH = 128
PICKED_PER_SHARD = 128
TOK_DEV = 2048
SLOT_CAPACITY = 512
SHARD_COUNT = 16
PICKED_OVERALL = 2048


def slot_positions(key):
    base_key = jax.random.fold_in(key, 11)
    shard_keys = jax.random.split(base_key, SHARD_COUNT)
    chosen = jax.vmap(lambda one_key: jax.random.permutation(one_key, TOK_DEV)[:SLOT_CAPACITY])(shard_keys)
    ordered = jnp.sort(chosen, axis=1) + (jnp.arange(SHARD_COUNT) * TOK_DEV)[:, None]
    return ordered.reshape(-1).astype(jnp.int32)


def draw_positions(key, part):
    return slot_positions(key)


def draw_q_home(key, part):
    count_of_rows = SHARD_COUNT * SLOT_CAPACITY
    value_rows = jnp.clip(2.5 * jax.random.normal(jax.random.fold_in(key, 23), (count_of_rows, QUERY_HEADS * HEAD_WIDTH), jnp.float32), -15.0, 15.0)
    return value_rows.astype(jnp.bfloat16)


def draw_k_home(key, part):
    count_of_rows = SHARD_COUNT * SLOT_CAPACITY
    value_rows = jnp.clip(jax.random.normal(jax.random.fold_in(key, 33), (count_of_rows, KEY_VALUE_HEADS * HEAD_WIDTH), jnp.float32), -6.0, 6.0)
    return value_rows.astype(jnp.bfloat16)


def block_scale(own_key, shape, cuts, least, top_value):
    gain, own = 1.0, jax.random.fold_in(own_key, 6)
    for position, shards_of in cuts:
        draws = jnp.exp(jax.random.uniform(jax.random.fold_in(own, position), (shards_of,), jnp.float32, least / len(cuts), top_value / len(cuts)))
        gain = gain * jnp.repeat(draws, shape[position] // shards_of).reshape([-1 if axis == position else 1 for axis in range(len(shape))])
    return gain


def split_up(count, total, reach, slope):
    portions = [(1 << 20) // math.isqrt(standing ** slope) + 1 for standing in range(2, count + 1)]
    rest, given = total - reach - (count - 1), [1] * (count - 1)
    while rest > 0:
        movable = [i for i in range(count - 1) if given[i] < reach]
        pool, left = sum([portions[i] for i in movable]), rest
        for i in movable:
            more = min(reach - given[i], max(1, left * portions[i] // pool), rest)
            given[i] = given[i] + more
            rest = rest - more
    return np.array([reach] + given)


def uneven(stream_key, count, total, bound, slope):
    if count == 2:
        one = jax.random.randint(stream_key, (), max(1, total - bound), min(bound, total - 1) + 1)
        return jnp.stack([one, total - one])
    tallies = jnp.asarray(split_up(count, total, bound, slope), jnp.int32)
    pairs = (count - 1) // 2
    donor, taker = tallies[1:1 + 2 * pairs:2], tallies[2:2 + 2 * pairs:2]
    room = jnp.minimum(donor - 1, bound - taker)
    moved = jax.random.randint(jax.random.fold_in(stream_key, 1), (pairs,), 0, 1 << 20) % (room + 1)
    tallies = tallies.at[1:1 + 2 * pairs:2].set(donor - moved).at[2:2 + 2 * pairs:2].set(taker + moved)
    return tallies[jax.random.permutation(jax.random.fold_in(stream_key, 2), count)]


def normal_values(own_key, dims, spread, most, shards=(), kind=jnp.bfloat16):
    factor_of = block_scale(own_key, dims, shards, -0.22, 0.18) if shards else 1.0
    array = jax.random.normal(own_key, dims, jnp.float32) * spread * factor_of
    return jnp.minimum(jnp.maximum(array, -most), most).astype(kind)


def setup_inputs(seed: int = 0) -> dict:
    keys = jax.random.split(jax.random.key(seed), 8)
    return {
        "q_home": draw_q_home(jax.random.fold_in(keys[7], 71), 0),
        "k_home": draw_k_home(jax.random.fold_in(keys[7], 71), 0),
        "value_slots_local": normal_values(keys[2], (SHARD_COUNT * SLOT_CAPACITY, KEY_VALUE_HEADS * HEAD_WIDTH), 3.0, 16.0, ((0, 16), (1, 2))),
        "out_weight": normal_values(keys[3], (QUERY_HEADS * HEAD_WIDTH, D), (QUERY_HEADS * HEAD_WIDTH) ** -0.5, 0.125, ((0, 2),)),
        "router": jnp.clip(jnp.exp(math.log(1.0) - 1.3862944 * jax.random.uniform(keys[4], (SHARD_COUNT * SLOT_CAPACITY,), jnp.float32) ** block_scale(keys[4], (SHARD_COUNT * SLOT_CAPACITY,), ((0, 16),), -0.2, 0.2)), 0.25, 1.0),
        "positions": draw_positions(jax.random.fold_in(keys[7], 71), 0),
        "counts": uneven(keys[6], SHARD_COUNT, PICKED_OVERALL, SLOT_CAPACITY, 2).astype(jnp.int32),
    }


rope_theta = 500000.0


def inverse_freqs():
    half_dim = HEAD_WIDTH // 2
    return rope_theta ** (-(jnp.arange(half_dim, dtype=jnp.float32) * 2.0 / HEAD_WIDTH))


def rotate_heads(value_rows, positions):
    heads = value_rows.shape[1] // HEAD_WIDTH
    half_dim = HEAD_WIDTH // 2
    inputs = value_rows.astype(jnp.float32).reshape(value_rows.shape[0], heads, HEAD_WIDTH)
    angles = positions.astype(jnp.float32)[:, None] * inverse_freqs()[None, :]
    cosine = jnp.cos(angles)[:, None, :]
    sine = jnp.sin(angles)[:, None, :]
    first = inputs[..., :half_dim]
    second = inputs[..., half_dim:]
    rotated = jnp.concatenate([first * cosine - second * sine, second * cosine + first * sine], axis=-1)
    return rotated.reshape(value_rows.shape).astype(jnp.bfloat16)


def reference(q_home, k_home, value_slots_local, out_weight, router, positions, counts):
    shard_total = counts.shape[0]
    offsets = (jnp.cumsum(counts) - counts).astype(jnp.int32)
    selected = jnp.arange(PICKED_OVERALL, dtype=jnp.int32)
    below = offsets[None, :] <= selected[:, None]
    source = (jnp.sum(below.astype(jnp.int32), axis=1) - 1).astype(jnp.int32)
    start_of = jnp.max(jnp.where(below, offsets[None, :], 0), axis=1).astype(jnp.int32)
    home_rows = (source * SLOT_CAPACITY + selected - start_of).astype(jnp.int32)
    sel_positions = jnp.take(positions, home_rows, axis=0)
    q_sel = rotate_heads(jnp.take(q_home, home_rows, axis=0), sel_positions)
    picked_keys = rotate_heads(jnp.take(k_home, home_rows, axis=0), sel_positions)
    picked_values = jnp.take(value_slots_local, home_rows, axis=0)
    group_width = QUERY_HEADS // KEY_VALUE_HEADS
    gathered_keys = picked_keys.astype(jnp.float32).reshape(PICKED_OVERALL, KEY_VALUE_HEADS, HEAD_WIDTH)
    gathered_values = picked_values.astype(jnp.float32).reshape(PICKED_OVERALL, KEY_VALUE_HEADS, HEAD_WIDTH)
    scale = 1.0 / (HEAD_WIDTH ** 0.5)

    def block_attend(block_index):
        first_row = block_index * PICKED_PER_SHARD
        query_block = lax.dynamic_slice_in_dim(q_sel, first_row, PICKED_PER_SHARD, 0)
        query_block = query_block.astype(jnp.float32).reshape(PICKED_PER_SHARD, KEY_VALUE_HEADS, group_width, HEAD_WIDTH)
        query_ids = first_row + jnp.arange(PICKED_PER_SHARD, dtype=jnp.int32)
        scores = jnp.einsum("bkgd,nkd->bkgn", query_block, gathered_keys) * scale
        visible = selected[None, None, None, :] <= query_ids[:, None, None, None]
        maxima = jnp.max(jnp.where(visible, scores, -1e30), axis=-1)
        exp_terms = jnp.where(visible, jnp.exp(scores - maxima[..., None]), 0.0)
        totals = jnp.sum(exp_terms, axis=-1)
        probs = lax.optimization_barrier(exp_terms.astype(jnp.bfloat16)).astype(jnp.float32)
        weighted = jnp.einsum("bkgn,nkd->bkgd", probs, gathered_values)
        attended_block = weighted / totals[..., None]
        return attended_block.reshape(PICKED_PER_SHARD, QUERY_HEADS * HEAD_WIDTH).astype(jnp.bfloat16)

    attended = lax.map(block_attend, jnp.arange(shard_total, dtype=jnp.int32))
    attended = attended.reshape(PICKED_OVERALL, QUERY_HEADS * HEAD_WIDTH)
    summed = jnp.dot(attended, out_weight, preferred_element_type=jnp.float32).astype(jnp.bfloat16)
    scaled = (jnp.take(router, home_rows, axis=0)[:, None] * summed.astype(jnp.float32)).astype(jnp.bfloat16)
    update = jnp.zeros((shard_total * SLOT_CAPACITY, D), jnp.bfloat16).at[home_rows].set(scaled)
    return update
```

```python
import functools
import math

import jax
import jax.numpy as jnp
from jax import lax
from jax.experimental import pallas as pl
from jax.experimental.pallas import tpu as pltpu
from jax.sharding import PartitionSpec as P

HEAD_WIDTH = 128
PICKED_PER_SHARD = 128
QUERY_BLOCK = 128
TILE = 16
SWAP_PARTS = 4
LANES = 128
COLUMN_TILE = 512
SPAN = 4
FAR = 1 << 28
LOW = -1e30
QUARTER = 1 << 30
SINE_TERMS = (
    6.283185159611168,
    -41.34165492934356,
    81.60099819261757,
    -76.54965682073457,
    39.53581371237487,
)

rope_theta = 500000.0


def turns_per_position():
    half = HEAD_WIDTH // 2
    turns = [rope_theta ** (-2.0 * i / HEAD_WIDTH) / (2.0 * math.pi) for i in range(half)]
    return [round(t * 4294967296.0) for t in turns]


def cosine_of(phase):
    fold = 0.25 - jnp.abs(phase.astype(jnp.float32) * (1.0 / 4294967296.0))
    square = fold * fold
    total = jnp.full_like(square, SINE_TERMS[-1])
    for term in SINE_TERMS[-2::-1]:
        total = total * square + term
    return total * fold


def turn(x, cosine, sine):
    return x * cosine + pltpu.roll(x, HEAD_WIDTH // 2, 1) * sine


def as_column(row):
    square = jnp.broadcast_to(row, (LANES, LANES))
    return square.T


def arrange(shards):
    side = 1 << ((shards.bit_length() - 1) // 3)
    return shards // (side * side), side * side


def plan(shards):
    lines, plane = arrange(shards)
    most = PICKED_PER_SHARD * lines + lines * (plane - 1) // 2
    room = -(-most // TILE) * TILE
    step = 96 if plane == 4 else 128
    sizes = [room % step] if room % step else []
    sizes += [step] * (room // step)
    return tuple(sizes)


def fused_kernel(
    shards,
    sizes,
    count_ref,
    pos_ref,
    router_ref,
    q_ref,
    k_ref,
    v_ref,
    weight_ref,
    out_ref,
    kin,
    q_in,
    pos_s,
    router_s,
    cos_s,
    sin_s,
    send,
    recv,
    inbox,
    kv,
    cnt_all,
    name_s,
    q_s,
    top_s,
    sum_s,
    acc_s,
    gain_s,
    own_w,
    got_w,
    mine_s,
    theirs_s,
    part_s,
    out_s,
    load_sem,
    cnt_sem,
    up_cnt_sem,
    deal_sem,
    up_sem,
    plane_sem,
    relay_sem,
    swap_sem,
    trade_sem,
    out_sem,
):
    lines, plane = arrange(shards)
    shift = plane.bit_length() - 1
    me = lax.axis_index("ctx")
    head = lax.axis_index("head")
    other = 1 - head
    z, spot = me // plane, me % plane
    square = plane == 4
    direct = (1, 2) if square else tuple(range(1, plane))
    pieces, _, deep, width = send.shape
    slots = q_in.shape[0]
    span = pieces * plane * deep
    blocks, groups, stack, _ = q_s.shape
    share = stack // QUERY_BLOCK
    keyed = k_ref.shape[1]
    half = own_w.shape[1]
    steps = len(sizes)
    firsts = [sum(sizes[:i]) for i in range(steps)]
    room = sum(sizes)
    factor = 1.4426950408889634 / HEAD_WIDTH**0.5

    count = count_ref[0]
    cnt_all[...] = jnp.zeros_like(cnt_all)
    cnt_all[me] = jnp.full(cnt_all.shape[1:], count, jnp.int32)

    barrier = pltpu.get_barrier_semaphore()
    for o in range(1, plane):
        pl.semaphore_signal(barrier, inc=1, device_id={"ctx": z * plane + (spot ^ o)})
    pl.semaphore_signal(barrier, inc=1, device_id={"head": other})

    @pl.when(z + 1 < lines)
    def _():
        pl.semaphore_signal(barrier, inc=1, device_id={"ctx": me + plane})

    @pl.when(z > 0)
    def _():
        pl.semaphore_signal(barrier, inc=1, device_id={"ctx": me - plane})

    loads = [
        pltpu.make_async_copy(pos_ref, pos_s, load_sem.at[0]),
        pltpu.make_async_copy(k_ref, kin.at[:, pl.ds(0, keyed)], load_sem.at[1]),
        pltpu.make_async_copy(v_ref, kin.at[:, pl.ds(keyed, keyed)], load_sem.at[2]),
        pltpu.make_async_copy(q_ref, q_in, load_sem.at[3]),
        pltpu.make_async_copy(router_ref, router_s, load_sem.at[4]),
        pltpu.make_async_copy(
            weight_ref.at[:, pl.ds(pl.multiple_of(head * half, half), half)],
            own_w,
            load_sem.at[5],
        ),
    ]
    for c in loads[:5]:
        c.start()

    lane = lax.broadcasted_iota(jnp.int32, (1, LANES), 1)
    rate = jnp.zeros((1, LANES), jnp.int32)
    for i, value in enumerate(turns_per_position()):
        rate = jnp.where((lane & (HEAD_WIDTH // 2 - 1)) == i, value, rate)
    lead = jnp.where(lane < HEAD_WIDTH // 2, QUARTER, -QUARTER)
    loads[0].wait()
    for b in range(blocks):
        at = pl.ds(b * QUERY_BLOCK, QUERY_BLOCK)
        column = as_column(pos_s[b : b + 1, :].astype(jnp.float32)).astype(jnp.int32)
        phase = column * rate
        cos_s[at, :] = cosine_of(phase)
        sin_s[at, :] = cosine_of(phase + lead)

    loads[1].wait()
    loads[2].wait()
    block = plane * deep
    row = lax.broadcasted_iota(jnp.int32, (block, block), 0)
    column = lax.broadcasted_iota(jnp.int32, (block, block), 1)
    chosen = column == plane * (row % deep) + row // deep
    deal_map = jnp.where(chosen, 1.0, 0.0).astype(jnp.bfloat16)
    for t in range(pieces):
        at = pl.ds(t * block, block)
        parts = []
        for c in range(keyed // HEAD_WIDTH):
            x = kin[at, pl.ds(c * HEAD_WIDTH, HEAD_WIDTH)].astype(jnp.float32)
            parts.append(turn(x, cos_s[at, :], sin_s[at, :]).astype(jnp.bfloat16))
        parts.append(kin[at, pl.ds(keyed, keyed)])
        rows = jnp.concatenate(parts, axis=1)
        dealt = jnp.dot(deal_map, rows, preferred_element_type=jnp.float32)
        send[t] = dealt.astype(jnp.bfloat16).reshape(plane, deep, width)

    greeted = plane + (z > 0).astype(jnp.int32) + (z + 1 < lines).astype(jnp.int32)
    pl.semaphore_wait(barrier, greeted)

    def mate(o):
        return {"ctx": z * plane + ((spot + o) & (plane - 1))}

    def remote(src, dst, sems, index, target):
        return pltpu.make_async_remote_copy(
            src_ref=src,
            dst_ref=dst,
            send_sem=sems.at[(0,) + index],
            recv_sem=sems.at[(1,) + index],
            device_id=target,
        )

    cnt_copies = [
        remote(cnt_all.at[me], cnt_all.at[me], cnt_sem, (o,), mate(o)) for o in range(1, plane)
    ]
    for c in cnt_copies:
        c.start()
    deals = [
        [
            remote(send.at[t, o], recv.at[t, spot], deal_sem, (t, o), mate(o))
            for o in range(1, plane)
        ]
        for t in range(pieces)
    ]
    for piece in deals:
        for c in piece:
            c.start()
    for t in range(pieces):
        recv[t, spot] = send[t, 0]
    depth = weight_ref.shape[0] // SWAP_PARTS
    columns = pl.ds(pl.multiple_of(other * half, half), half)
    swaps = []
    for i in range(SWAP_PARTS):
        at = pl.ds(i * depth, depth)
        swaps.append(
            remote(
                weight_ref.at[at, columns], got_w.at[at, :], swap_sem, (i,), {"head": other}
            )
        )
    for c in swaps:
        c.start()
    loads[5].start()

    loads[3].wait()

    @pl.loop(0, blocks)
    def _(b):
        top_s[b] = jnp.full_like(top_s[b], LOW)
        sum_s[b] = jnp.zeros_like(sum_s[b])
        acc_s[b] = jnp.zeros_like(acc_s[b])
        at = pl.ds(pl.multiple_of(b * QUERY_BLOCK, QUERY_BLOCK), QUERY_BLOCK)
        cosine, sine = cos_s[at, :] * factor, sin_s[at, :] * factor
        for g in range(groups):
            for h in range(share):
                x = q_in[at, pl.ds((g * share + h) * HEAD_WIDTH, HEAD_WIDTH)].astype(jnp.float32)
                q_s[b, g, pl.ds(h * QUERY_BLOCK, QUERY_BLOCK), :] = turn(x, cosine, sine).astype(
                    jnp.bfloat16
                )

    def table_rows(p):
        return cnt_all.at[pl.ds(p * plane, plane)]

    def up_counts(far):
        rows = table_rows(z - far)
        return remote(rows, rows, up_cnt_sem, (far + 1,), {"ctx": me + plane})

    def up_counts_in(far):
        rows = table_rows(z - far)
        return remote(rows, rows, up_cnt_sem, (far,), {"ctx": me - plane})

    for c in cnt_copies:
        c.wait_recv()
    pl.when(z + 1 < lines)(lambda: up_counts(0).start())
    for far in range(1, lines):

        @pl.when(z >= far)
        def _():
            up_counts_in(far).wait_recv()
            if far + 1 < lines:
                pl.when(z + 1 < lines)(lambda: up_counts(far).start())

    def dealt_to(line, counts, source):
        skip = (line - source) & (plane - 1)
        return (counts + (plane - 1) - skip) >> shift, skip

    counts = cnt_all[:, 0, :]
    shard_row = lax.broadcasted_iota(jnp.int32, counts.shape, 0)
    held, _ = dealt_to(spot, counts, shard_row)
    below = jnp.sum(jnp.where(shard_row < z * plane, held, 0), axis=0, keepdims=True)
    segments = pieces * plane
    seg = lax.broadcasted_iota(jnp.int32, (segments, LANES), 0)
    seg_held = jnp.zeros((segments, LANES), jnp.int32)
    for s in range(plane):
        mine = jnp.broadcast_to(cnt_all[z * plane + s, 0:1, :], seg.shape)
        seg_held = jnp.where((seg & (plane - 1)) == s, mine, seg_held)
    seg_held, _ = dealt_to(spot, seg_held, seg)
    seg_held = jnp.clip(seg_held - deep * (seg >> shift), 0, deep)
    seg_start = jnp.broadcast_to(below, seg.shape)
    for e in range(segments - 1):
        seg_start += jnp.where(seg > e, seg_held[e : e + 1, :], 0)
    wide = (segments, span)
    wide_held = jnp.broadcast_to(seg_held[:, :1], wide)
    wide_start = jnp.broadcast_to(seg_start[:, :1], wide)
    within = lax.broadcasted_iota(jnp.int32, wide, 1) - deep * lax.broadcasted_iota(
        jnp.int32, wide, 0
    )
    live = (within >= 0) & (within < wide_held)
    target = jnp.sum(jnp.where(live, wide_start + within + 1, 0), axis=0, keepdims=True) - 1

    arrived = [0]

    def region(k, line):
        start = plane * firsts[k] + line * sizes[k]
        return pl.ds(pl.multiple_of(start, TILE), sizes[k])

    def place(k):
        last = firsts[k] + sizes[k]
        needed = min(pieces, -(-last // deep))
        while arrived[0] < needed:
            for c in deals[arrived[0]]:
                c.wait_recv()
            arrived[0] += 1
        used = needed * plane * deep
        spots = lax.broadcasted_iota(jnp.int32, (sizes[k], used), 0) + firsts[k]
        pick = jnp.where(spots == target[:, :used], 1.0, 0.0).astype(jnp.bfloat16)
        rows = recv[pl.ds(0, needed)].reshape(used, width)
        kv[region(k, spot), :] = jnp.dot(pick, rows, preferred_element_type=jnp.float32).astype(
            jnp.bfloat16
        )

    def inner(k):
        return pl.ds(firsts[k], sizes[k])

    def up(k):
        return remote(
            kv.at[region(k, spot), :], inbox.at[inner(k), :], up_sem, (k,), {"ctx": me + plane}
        )

    def up_in(k):
        here = inbox.at[inner(k), :]
        return remote(here, here, up_sem, (k,), {"ctx": me - plane})

    def across(k, o):
        here = kv.at[region(k, spot), :]
        return remote(here, here, plane_sem, (k, o), {"ctx": z * plane + (spot ^ o)})

    def across_in(k, o):
        here = kv.at[region(k, spot ^ o), :]
        return remote(here, here, plane_sem, (k, o), {"ctx": z * plane + (spot ^ o)})

    def relay(k, part, peer):
        here = kv.at[region(k, spot ^ peer), pl.ds(part * keyed, keyed)]
        return remote(
            here, here, relay_sem, (k, part), {"ctx": z * plane + (spot ^ (3 - peer))}
        )

    def relay_in(k, part):
        here = kv.at[region(k, spot ^ 3), pl.ds(part * keyed, keyed)]
        return remote(here, here, relay_sem, (k, part), {"ctx": z * plane + (spot ^ 3)})

    def merge(k):
        @pl.when(z > 0)
        def _():
            up_in(k).wait_recv()
            kv[region(k, spot), :] += inbox[inner(k), :]

        @pl.when(z + 1 < lines)
        def _():
            up(k).start()

        for o in direct:
            across(k, o).start()

    def pass_on(k):
        for o in direct:
            across_in(k, o).wait_recv()
        if square:
            for part, peer in ((0, 1), (1, 2)):
                relay(k, part, peer).start()

    def complete(k):
        if square:
            for part in range(2):
                relay_in(k, part).wait_recv()

    ranks = lines * pieces * plane
    lanes = -(-ranks // LANES) * LANES

    def make_names():
        e = lax.broadcasted_iota(jnp.int32, (1, lanes), 1)
        source = e & (plane - 1)
        piece = (e >> shift) & (pieces - 1)
        level = e >> (shift + pieces.bit_length() - 1)
        shard = level * plane + source
        total = jnp.zeros((1, lanes), jnp.int32)
        for d in range(shards):
            number = cnt_all[d, 0:1, :]
            number = jnp.concatenate([number] * (lanes // LANES), axis=1)
            total = jnp.where(shard == d, number, total)
        earlier = jnp.where(
            lax.broadcasted_iota(jnp.int32, (lanes, lanes), 0)
            < lax.broadcasted_iota(jnp.int32, (lanes, lanes), 1),
            1.0,
            0.0,
        ).astype(jnp.bfloat16)
        for line in range(plane):
            mine, skip = dealt_to(line, total, source)
            mine = jnp.clip(mine - deep * piece, 0, deep)
            mine = jnp.where(level <= z, mine, 0)
            start = jnp.dot(
                jnp.broadcast_to(mine.astype(jnp.float32), (8, lanes)).astype(jnp.bfloat16),
                earlier,
                preferred_element_type=jnp.float32,
            )[:1].astype(jnp.int32)
            first_name = shard * slots + plane * deep * piece + skip
            for k in range(steps):
                shape = (sizes[k], lanes)
                within = lax.broadcasted_iota(jnp.int32, shape, 0) + (firsts[k] - start)
                live = (within >= 0) & (within < mine)
                names = jnp.min(
                    jnp.where(live, first_name + plane * within, FAR), axis=1, keepdims=True
                )
                name_s[pl.ds(plane * firsts[k] + line * sizes[k], sizes[k]), :] = jnp.broadcast_to(
                    names, (sizes[k], LANES)
                )

    def attend(k):
        rows = SPAN * sizes[k]

        @pl.loop(0, blocks * (plane // SPAN))
        def _(i):
            b, part = i % blocks, i // blocks
            at = pl.ds(pl.multiple_of(plane * firsts[k] + part * rows, TILE), rows)
            query = me * slots + b * QUERY_BLOCK
            query = query + lax.broadcasted_iota(jnp.int32, (rows, QUERY_BLOCK), 1)
            bias = jnp.where(name_s[at, :] <= query, 0.0, LOW)
            bias = jnp.concatenate([bias] * share, axis=1)
            scores = []
            for g in range(groups):
                key = kv[at, pl.ds(g * HEAD_WIDTH, HEAD_WIDTH)]
                scores.append(
                    lax.dot_general(
                        key, q_s[b, g], (((1,), (1,)), ((), ())), preferred_element_type=jnp.float32
                    )
                    + bias
                )
            for g in range(groups):
                value = kv[at, pl.ds((groups + g) * HEAD_WIDTH, HEAD_WIDTH)]
                old = top_s[b, g]
                top = jnp.maximum(old, jnp.max(scores[g], axis=0, keepdims=True))
                terms = jnp.exp2(scores[g] - top)
                rescale = jnp.exp2(old - top)
                top_s[b, g] = top
                sum_s[b, g] = sum_s[b, g] * rescale + jnp.sum(terms, axis=0, keepdims=True)
                acc_s[b, g] = acc_s[b, g] * rescale + lax.dot_general(
                    value,
                    terms.astype(jnp.bfloat16),
                    (((0,), (0,)), ((), ())),
                    preferred_element_type=jnp.float32,
                )

    place(0)
    for k in range(steps):
        merge(k)
        if k + 1 < steps:
            place(k + 1)
        if k == 0:
            make_names()
        if k >= 1:
            pass_on(k - 1)
        if k >= 2:
            complete(k - 2)
            attend(k - 2)
    pass_on(steps - 1)
    for k in (steps - 2, steps - 1):
        complete(k)
        attend(k)

    loads[4].wait()
    for b in range(blocks):
        at = pl.ds(b * QUERY_BLOCK, QUERY_BLOCK)
        live = b * QUERY_BLOCK + lax.broadcasted_iota(jnp.int32, (LANES, LANES), 0) < count
        gain_s[at, :] = jnp.where(live, as_column(router_s[b : b + 1, :]), 0.0)

    def trade(b):
        at = pl.ds(b * QUERY_BLOCK, QUERY_BLOCK)
        return remote(mine_s.at[at, :], theirs_s.at[at, :], trade_sem, (b,), {"head": other})

    for b in range(blocks):
        at = pl.ds(b * QUERY_BLOCK, QUERY_BLOCK)
        for g in range(groups):
            done = acc_s[b, g] / sum_s[b, g]
            for h in range(share):
                part = done[:, h * QUERY_BLOCK : (h + 1) * QUERY_BLOCK]
                mine_s[at, pl.ds((g * share + h) * HEAD_WIDTH, HEAD_WIDTH)] = part.T.astype(
                    jnp.bfloat16
                )
        trade(b).start()

    tile = min(COLUMN_TILE, half)
    tiles = half // tile
    loads[5].wait()

    @pl.loop(0, tiles)
    def _(n):
        cols = pl.ds(pl.multiple_of(n * tile, tile), tile)
        part_s[:, cols] = jnp.dot(mine_s[...], own_w[:, cols], preferred_element_type=jnp.float32)

    for c in swaps:
        c.wait_recv()
    for b in range(blocks):
        trade(b).wait_recv()
    gain = jnp.concatenate([gain_s[...]] * (tile // LANES), axis=1)
    outs = []
    for n in range(tiles):
        cols = pl.ds(n * tile, tile)
        summed = part_s[:, cols] + jnp.dot(
            theirs_s[...], got_w[:, cols], preferred_element_type=jnp.float32
        )
        summed = summed.astype(jnp.bfloat16).astype(jnp.float32)
        out_s[:, cols] = (gain * summed).astype(jnp.bfloat16)
        outs.append(pltpu.make_async_copy(out_s.at[:, cols], out_ref.at[:, cols], out_sem.at[n]))
        outs[n].start()

    for c in cnt_copies:
        c.wait_send()
    for far in range(lines - 1):
        pl.when((z >= far) & (z + 1 < lines))(lambda: up_counts(far).wait_send())
    for piece in deals:
        for c in piece:
            c.wait_send()
    for k in range(steps):
        pl.when(z + 1 < lines)(lambda: up(k).wait_send())
        for o in direct:
            across(k, o).wait_send()
        if square:
            for part, peer in ((0, 1), (1, 2)):
                relay(k, part, peer).wait_send()
    for c in swaps:
        c.wait_send()
    for b in range(blocks):
        trade(b).wait_send()
    for c in outs:
        c.wait()


def local(q_home, k_home, value_slots_local, out_weight, router, positions, counts):
    shards = lax.axis_size("ctx")
    lines, plane = arrange(shards)
    sizes = plan(shards)
    steps, room = len(sizes), sum(sizes)
    slots, features = q_home.shape
    keyed = k_home.shape[1]
    width = 2 * keyed
    groups = keyed // HEAD_WIDTH
    share = features // HEAD_WIDTH // groups
    stack = share * QUERY_BLOCK
    blocks = slots // QUERY_BLOCK
    half = out_weight.shape[1] // 2
    deep = max(TILE, QUERY_BLOCK // plane)
    pieces = slots // (deep * plane)
    tiles = half // min(COLUMN_TILE, half)
    rows = lambda a: a.reshape(blocks, QUERY_BLOCK)
    vmem, dma = pltpu.VMEM, pltpu.SemaphoreType.DMA
    bf16, f32, i32 = jnp.bfloat16, jnp.float32, jnp.int32
    return pl.pallas_call(
        functools.partial(fused_kernel, shards, sizes),
        out_shape=jax.ShapeDtypeStruct((slots, half), bf16),
        in_specs=[pl.BlockSpec(memory_space=pltpu.SMEM)] + [pl.BlockSpec(memory_space=pl.ANY)] * 6,
        out_specs=pl.BlockSpec(memory_space=pl.ANY),
        scratch_shapes=[
            vmem((slots, width), bf16),
            vmem((slots, features), bf16),
            vmem((blocks, QUERY_BLOCK), i32),
            vmem((blocks, QUERY_BLOCK), f32),
            vmem((slots, HEAD_WIDTH), f32),
            vmem((slots, HEAD_WIDTH), f32),
            vmem((pieces, plane, deep, width), bf16),
            vmem((pieces, plane, deep, width), bf16),
            vmem((room, width), bf16),
            vmem((plane * room, width), bf16),
            vmem((shards, 8, LANES), i32),
            vmem((plane * room, LANES), i32),
            vmem((blocks, groups, stack, HEAD_WIDTH), bf16),
            vmem((blocks, groups, 1, stack), f32),
            vmem((blocks, groups, 1, stack), f32),
            vmem((blocks, groups, HEAD_WIDTH, stack), f32),
            vmem((slots, LANES), f32),
            vmem((features, half), bf16),
            vmem((features, half), bf16),
            vmem((slots, features), bf16),
            vmem((slots, features), bf16),
            vmem((slots, half), f32),
            vmem((slots, half), bf16),
            dma((6,)),
            dma((2, plane)),
            dma((2, lines)),
            dma((2, pieces, plane)),
            dma((2, steps)),
            dma((2, steps, plane)),
            dma((2, steps, 2)),
            dma((2, SWAP_PARTS)),
            dma((2, blocks)),
            dma((tiles,)),
        ],
        compiler_params=pltpu.CompilerParams(collective_id=0, has_side_effects=True),
        name="fused",
    )(
        counts,
        rows(positions),
        rows(router),
        q_home,
        k_home,
        value_slots_local,
        out_weight,
    )


def solution(mesh):
    return jax.shard_map(
        local,
        mesh=mesh,
        in_specs=(
            P("ctx", "head"),
            P("ctx", "head"),
            P("ctx", "head"),
            P("head", None),
            P("ctx"),
            P("ctx"),
            P("ctx"),
        ),
        out_specs=P("ctx", "head"),
        check_vma=False,
    )
```

```python
import functools
import math

import jax
import jax.numpy as jnp
from jax import lax
from jax.experimental import pallas as pl
from jax.experimental.pallas import tpu as pltpu
from jax.sharding import PartitionSpec as P

HEAD_WIDTH = 128
PICKED_PER_SHARD = 128
QUERY_BLOCK = 128
TILE = 16
SWAP_PARTS = 4
LANES = 128
COLUMN_TILE = 512
SPAN = 4
STEP = 48
PASS_LAG = 3
DONE_LAG = 3
SPARE = 10 << 20
FAR = 1 << 28
LOW = -1e30
QUARTER = 1 << 30
SINE_TERMS = (
    6.283185159611168,
    -41.34165492934356,
    81.60099819261757,
    -76.54965682073457,
    39.53581371237487,
)

rope_theta = 500000.0


def turns_per_position():
    half = HEAD_WIDTH // 2
    turns = [rope_theta ** (-2.0 * i / HEAD_WIDTH) / (2.0 * math.pi) for i in range(half)]
    return [round(t * 4294967296.0) for t in turns]


def cosine_of(phase):
    fold = 0.25 - jnp.abs(phase.astype(jnp.float32) * (1.0 / 4294967296.0))
    square = fold * fold
    total = jnp.full_like(square, SINE_TERMS[-1])
    for term in SINE_TERMS[-2::-1]:
        total = total * square + term
    return total * fold


def turn(x, cosine, sine):
    return x * cosine + pltpu.roll(x, HEAD_WIDTH // 2, 1) * sine


def as_column(row):
    square = jnp.broadcast_to(row, (LANES, LANES))
    return square.T


def arrange(shards):
    side = 1 << ((shards.bit_length() - 1) // 3)
    return shards // (side * side), side * side


def plan(shards):
    lines, plane = arrange(shards)
    most = PICKED_PER_SHARD * lines + lines * (plane - 1) // 2
    room = -(-most // TILE) * TILE
    step = STEP if plane == SPAN else 2 * STEP
    sizes = []
    while sum(sizes) < room:
        grown = TILE << len(sizes) if plane == SPAN else step
        sizes.append(min(grown, step, room - sum(sizes)))
    return tuple(sizes)


def gather_up(sizes):
    most = 2 * STEP if len(sizes) > 2 and max(sizes) <= STEP else max(sizes)
    groups, held = [], []
    for k, size in enumerate(sizes):
        if held and (sum(sizes[i] for i in held) + size > most or k == len(sizes) - 1):
            groups.append(held)
            held = []
        held.append(k)
    return groups + [held]


def fused_kernel(
    shards,
    sizes,
    count_ref,
    pos_ref,
    router_ref,
    q_ref,
    k_ref,
    v_ref,
    weight_ref,
    out_ref,
    kin,
    q_in,
    pos_s,
    router_s,
    cos_s,
    sin_s,
    send,
    recv,
    inbox,
    kv,
    cnt_all,
    name_s,
    q_s,
    top_s,
    sum_s,
    acc_s,
    gain_s,
    own_w,
    got_w,
    mine_s,
    theirs_s,
    part_s,
    load_sem,
    cnt_sem,
    up_cnt_sem,
    deal_sem,
    up_sem,
    plane_sem,
    relay_sem,
    swap_sem,
    trade_sem,
    ):
    lines, plane = arrange(shards)
    shift = plane.bit_length() - 1
    me = lax.axis_index("ctx")
    head = lax.axis_index("head")
    other = 1 - head
    z, spot = me // plane, me % plane
    square = plane == 4
    direct = (1, 2) if square else tuple(range(1, plane))
    pieces, _, deep, width = send.shape
    slots = q_in.shape[0]
    span = pieces * plane * deep
    blocks, groups, stack, _ = q_s.shape
    share = stack // QUERY_BLOCK
    keyed = k_ref.shape[1]
    half = own_w.shape[1]
    steps = len(sizes)
    firsts = [sum(sizes[:i]) for i in range(steps)]
    room = sum(sizes)
    factor = 1.4426950408889634 / HEAD_WIDTH**0.5

    count = count_ref[0]
    cnt_all[...] = jnp.zeros_like(cnt_all)
    cnt_all[me] = jnp.full(cnt_all.shape[1:], count, jnp.int32)

    barrier = pltpu.get_barrier_semaphore()
    for o in range(1, plane):
        pl.semaphore_signal(barrier, inc=1, device_id={"ctx": z * plane + (spot ^ o)})
    pl.semaphore_signal(barrier, inc=1, device_id={"head": other})

    @pl.when(z + 1 < lines)
    def _():
        pl.semaphore_signal(barrier, inc=1, device_id={"ctx": me + plane})

    @pl.when(z > 0)
    def _():
        pl.semaphore_signal(barrier, inc=1, device_id={"ctx": me - plane})

    loads = [
        pltpu.make_async_copy(pos_ref, pos_s, load_sem.at[0]),
        pltpu.make_async_copy(k_ref, kin.at[:, pl.ds(0, keyed)], load_sem.at[1]),
        pltpu.make_async_copy(v_ref, kin.at[:, pl.ds(keyed, keyed)], load_sem.at[2]),
        pltpu.make_async_copy(q_ref, q_in, load_sem.at[3]),
        pltpu.make_async_copy(router_ref, router_s, load_sem.at[4]),
        pltpu.make_async_copy(
            weight_ref.at[:, pl.ds(pl.multiple_of(head * half, half), half)],
            own_w,
            load_sem.at[5],
        ),
    ]
    for c in loads[:5]:
        c.start()

    lane = lax.broadcasted_iota(jnp.int32, (1, LANES), 1)
    rate = jnp.zeros((1, LANES), jnp.int32)
    for i, value in enumerate(turns_per_position()):
        rate = jnp.where((lane & (HEAD_WIDTH // 2 - 1)) == i, value, rate)
    lead = jnp.where(lane < HEAD_WIDTH // 2, QUARTER, -QUARTER)
    loads[0].wait()
    for b in range(blocks):
        at = pl.ds(b * QUERY_BLOCK, QUERY_BLOCK)
        column = as_column(pos_s[b : b + 1, :].astype(jnp.float32)).astype(jnp.int32)
        phase = column * rate
        cos_s[at, :] = cosine_of(phase)
        sin_s[at, :] = cosine_of(phase + lead)

    loads[1].wait()
    loads[2].wait()
    block = plane * deep
    row = lax.broadcasted_iota(jnp.int32, (block, block), 0)
    column = lax.broadcasted_iota(jnp.int32, (block, block), 1)
    chosen = column == plane * (row % deep) + row // deep
    deal_map = jnp.where(chosen, 1.0, 0.0).astype(jnp.bfloat16)
    for t in range(pieces):
        at = pl.ds(t * block, block)
        parts = []
        for c in range(keyed // HEAD_WIDTH):
            x = kin[at, pl.ds(c * HEAD_WIDTH, HEAD_WIDTH)].astype(jnp.float32)
            parts.append(turn(x, cos_s[at, :], sin_s[at, :]).astype(jnp.bfloat16))
        parts.append(kin[at, pl.ds(keyed, keyed)])
        rows = jnp.concatenate(parts, axis=1)
        dealt = jnp.dot(deal_map, rows, preferred_element_type=jnp.float32)
        send[t] = dealt.astype(jnp.bfloat16).reshape(plane, deep, width)

    greeted = plane + (z > 0).astype(jnp.int32) + (z + 1 < lines).astype(jnp.int32)
    pl.semaphore_wait(barrier, greeted)

    def mate(o):
        return {"ctx": z * plane + ((spot + o) & (plane - 1))}

    def remote(src, dst, sems, index, target):
        return pltpu.make_async_remote_copy(
            src_ref=src,
            dst_ref=dst,
            send_sem=sems.at[(0,) + index],
            recv_sem=sems.at[(1,) + index],
            device_id=target,
        )

    cnt_copies = [
        remote(cnt_all.at[me], cnt_all.at[me], cnt_sem, (o,), mate(o)) for o in range(1, plane)
    ]
    for c in cnt_copies:
        c.start()
    deals = [
        [
            remote(send.at[t, o], recv.at[t, spot], deal_sem, (t, o), mate(o))
            for o in range(1, plane)
        ]
        for t in range(pieces)
    ]
    for piece in deals:
        for c in piece:
            c.start()
    for t in range(pieces):
        recv[t, spot] = send[t, 0]
    depth = weight_ref.shape[0] // SWAP_PARTS
    columns = pl.ds(pl.multiple_of(other * half, half), half)
    swaps = []
    for i in range(SWAP_PARTS):
        at = pl.ds(i * depth, depth)
        swaps.append(
            remote(
                weight_ref.at[at, columns], got_w.at[at, :], swap_sem, (i,), {"head": other}
            )
        )
    for c in swaps:
        c.start()
    loads[5].start()

    loads[3].wait()

    @pl.loop(0, blocks)
    def _(b):
        top_s[b] = jnp.full_like(top_s[b], LOW)
        sum_s[b] = jnp.zeros_like(sum_s[b])
        acc_s[b] = jnp.zeros_like(acc_s[b])
        at = pl.ds(pl.multiple_of(b * QUERY_BLOCK, QUERY_BLOCK), QUERY_BLOCK)
        cosine, sine = cos_s[at, :] * factor, sin_s[at, :] * factor
        for g in range(groups):
            for h in range(share):
                x = q_in[at, pl.ds((g * share + h) * HEAD_WIDTH, HEAD_WIDTH)].astype(jnp.float32)
                q_s[b, g, pl.ds(h * QUERY_BLOCK, QUERY_BLOCK), :] = turn(x, cosine, sine).astype(
                    jnp.bfloat16
                )

    def table_rows(p):
        return cnt_all.at[pl.ds(p * plane, plane)]

    def up_counts(far):
        rows = table_rows(z - far)
        return remote(rows, rows, up_cnt_sem, (far + 1,), {"ctx": me + plane})

    def up_counts_in(far):
        rows = table_rows(z - far)
        return remote(rows, rows, up_cnt_sem, (far,), {"ctx": me - plane})

    for c in cnt_copies:
        c.wait_recv()
    pl.when(z + 1 < lines)(lambda: up_counts(0).start())
    for far in range(1, lines):

        @pl.when(z >= far)
        def _():
            up_counts_in(far).wait_recv()
            if far + 1 < lines:
                pl.when(z + 1 < lines)(lambda: up_counts(far).start())

    def dealt_to(line, counts, source):
        skip = (line - source) & (plane - 1)
        return (counts + (plane - 1) - skip) >> shift, skip

    counts = cnt_all[:, 0, :]
    shard_row = lax.broadcasted_iota(jnp.int32, counts.shape, 0)
    held, _ = dealt_to(spot, counts, shard_row)
    below = jnp.sum(jnp.where(shard_row < z * plane, held, 0), axis=0, keepdims=True)
    segments = pieces * plane
    seg = lax.broadcasted_iota(jnp.int32, (segments, LANES), 0)
    seg_held = jnp.zeros((segments, LANES), jnp.int32)
    for s in range(plane):
        mine = jnp.broadcast_to(cnt_all[z * plane + s, 0:1, :], seg.shape)
        seg_held = jnp.where((seg & (plane - 1)) == s, mine, seg_held)
    seg_held, _ = dealt_to(spot, seg_held, seg)
    seg_held = jnp.clip(seg_held - deep * (seg >> shift), 0, deep)
    seg_start = jnp.broadcast_to(below, seg.shape)
    for e in range(segments - 1):
        seg_start += jnp.where(seg > e, seg_held[e : e + 1, :], 0)
    wide = (segments, span)
    wide_held = jnp.broadcast_to(seg_held[:, :1], wide)
    wide_start = jnp.broadcast_to(seg_start[:, :1], wide)
    within = lax.broadcasted_iota(jnp.int32, wide, 1) - deep * lax.broadcasted_iota(
        jnp.int32, wide, 0
    )
    live = (within >= 0) & (within < wide_held)
    target = jnp.sum(jnp.where(live, wide_start + within + 1, 0), axis=0, keepdims=True) - 1

    arrived = [0]

    def region(k, line):
        start = plane * firsts[k] + line * sizes[k]
        return pl.ds(pl.multiple_of(start, TILE), sizes[k])

    def place(k):
        last = firsts[k] + sizes[k]
        needed = min(pieces, -(-last // deep))
        while arrived[0] < needed:
            for c in deals[arrived[0]]:
                c.wait_recv()
            arrived[0] += 1
        used = needed * plane * deep
        spots = lax.broadcasted_iota(jnp.int32, (sizes[k], used), 0) + firsts[k]
        pick = jnp.where(spots == target[:, :used], 1.0, 0.0).astype(jnp.bfloat16)
        rows = recv[pl.ds(0, needed)].reshape(used, width)
        kv[region(k, spot), :] = jnp.dot(pick, rows, preferred_element_type=jnp.float32).astype(
            jnp.bfloat16
        )

    def inner(k):
        return pl.ds(firsts[k], sizes[k])

    def up(k):
        return remote(
            kv.at[region(k, spot), :], inbox.at[inner(k), :], up_sem, (k,), {"ctx": me + plane}
        )

    def up_in(k):
        here = inbox.at[inner(k), :]
        return remote(here, here, up_sem, (k,), {"ctx": me - plane})

    def across(k, o):
        here = kv.at[region(k, spot), :]
        return remote(here, here, plane_sem, (k, o), {"ctx": z * plane + (spot ^ o)})

    def across_in(k, o):
        here = kv.at[region(k, spot ^ o), :]
        return remote(here, here, plane_sem, (k, o), {"ctx": z * plane + (spot ^ o)})

    def relay(k, part, peer):
        here = kv.at[region(k, spot ^ peer), pl.ds(part * keyed, keyed)]
        return remote(
            here, here, relay_sem, (k, part), {"ctx": z * plane + (spot ^ (3 - peer))}
        )

    def relay_in(k, part):
        here = kv.at[region(k, spot ^ 3), pl.ds(part * keyed, keyed)]
        return remote(here, here, relay_sem, (k, part), {"ctx": z * plane + (spot ^ 3)})

    def merge(k):
        @pl.when(z > 0)
        def _():
            up_in(k).wait_recv()
            kv[region(k, spot), :] += inbox[inner(k), :]

        @pl.when(z + 1 < lines)
        def _():
            up(k).start()

        for o in direct:
            across(k, o).start()

    def pass_on(k):
        for o in direct:
            across_in(k, o).wait_recv()
        if square:
            for part, peer in ((0, 1), (1, 2)):
                relay(k, part, peer).start()

    def complete(k):
        if square:
            for part in range(2):
                relay_in(k, part).wait_recv()

    ranks = lines * pieces * plane
    lanes = -(-ranks // LANES) * LANES

    def make_names():
        e = lax.broadcasted_iota(jnp.int32, (1, lanes), 1)
        source = e & (plane - 1)
        piece = (e >> shift) & (pieces - 1)
        level = e >> (shift + pieces.bit_length() - 1)
        shard = level * plane + source
        total = jnp.zeros((1, lanes), jnp.int32)
        for d in range(shards):
            number = cnt_all[d, 0:1, :]
            number = jnp.concatenate([number] * (lanes // LANES), axis=1)
            total = jnp.where(shard == d, number, total)
        earlier = jnp.where(
            lax.broadcasted_iota(jnp.int32, (lanes, lanes), 0)
            < lax.broadcasted_iota(jnp.int32, (lanes, lanes), 1),
            1.0,
            0.0,
        ).astype(jnp.bfloat16)
        for line in range(plane):
            mine, skip = dealt_to(line, total, source)
            mine = jnp.clip(mine - deep * piece, 0, deep)
            mine = jnp.where(level <= z, mine, 0)
            start = jnp.dot(
                jnp.broadcast_to(mine.astype(jnp.float32), (8, lanes)).astype(jnp.bfloat16),
                earlier,
                preferred_element_type=jnp.float32,
            )[:1].astype(jnp.int32)
            first_name = shard * slots + plane * deep * piece + skip
            for k in range(steps):
                shape = (sizes[k], lanes)
                within = lax.broadcasted_iota(jnp.int32, shape, 0) + (firsts[k] - start)
                live = (within >= 0) & (within < mine)
                names = jnp.min(
                    jnp.where(live, first_name + plane * within, FAR), axis=1, keepdims=True
                )
                name_s[pl.ds(plane * firsts[k] + line * sizes[k], sizes[k]), :] = jnp.broadcast_to(
                    names, (sizes[k], LANES)
                )

    def attend(members, final=False):
        rows = SPAN * sum(sizes[k] for k in members)
        parts = plane // SPAN

        @pl.loop(0, blocks * parts)
        def _(i):
            b, part = i % blocks, i // blocks
            at = pl.ds(pl.multiple_of(plane * firsts[members[0]] + part * rows, TILE), rows)
            query = me * slots + b * QUERY_BLOCK
            query = query + lax.broadcasted_iota(jnp.int32, (rows, QUERY_BLOCK), 1)
            bias = jnp.where(name_s[at, :] <= query, 0.0, LOW)
            bias = jnp.concatenate([bias] * share, axis=1)
            scores = []
            for g in range(groups):
                key = kv[at, pl.ds(g * HEAD_WIDTH, HEAD_WIDTH)]
                scores.append(
                    lax.dot_general(
                        key, q_s[b, g], (((1,), (1,)), ((), ())), preferred_element_type=jnp.float32
                    )
                    + bias
                )
            for g in range(groups):
                value = kv[at, pl.ds((groups + g) * HEAD_WIDTH, HEAD_WIDTH)]
                old = top_s[b, g]
                top = jnp.maximum(old, jnp.max(scores[g], axis=0, keepdims=True))
                terms = jnp.exp2(scores[g] - top)
                rescale = jnp.exp2(old - top)
                top_s[b, g] = top
                sum_s[b, g] = sum_s[b, g] * rescale + jnp.sum(terms, axis=0, keepdims=True)
                acc_s[b, g] = acc_s[b, g] * rescale + lax.dot_general(
                    value,
                    terms.astype(jnp.bfloat16),
                    (((0,), (0,)), ((), ())),
                    preferred_element_type=jnp.float32,
                )
            if final:
                pl.when(part == parts - 1)(functools.partial(finish, b))

    def block_rows(b):
        return pl.ds(pl.multiple_of(b * QUERY_BLOCK, QUERY_BLOCK), QUERY_BLOCK)

    def trade(b):
        at = block_rows(b)
        return remote(mine_s.at[at, :], theirs_s.at[at, :], trade_sem, (b,), {"head": other})

    def finish(b):
        for g in range(groups):
            done = acc_s[b, g] / sum_s[b, g]
            for h in range(share):
                part = done[:, h * QUERY_BLOCK : (h + 1) * QUERY_BLOCK]
                cols = pl.ds((g * share + h) * HEAD_WIDTH, HEAD_WIDTH)
                mine_s[block_rows(b), cols] = part.T.astype(jnp.bfloat16)
        trade(b).start()

    loads[4].wait()
    for b in range(blocks):
        at = pl.ds(b * QUERY_BLOCK, QUERY_BLOCK)
        live = b * QUERY_BLOCK + lax.broadcasted_iota(jnp.int32, (LANES, LANES), 0) < count
        gain_s[at, :] = jnp.where(live, as_column(router_s[b : b + 1, :]), 0.0)

    place(0)
    pl.when(z > 0)(make_names)
    waiting = gather_up(sizes)
    completed = [0]

    def attend_ready(upto):
        while waiting and waiting[0][-1] <= upto:
            members = waiting.pop(0)
            while completed[0] <= members[-1]:
                complete(completed[0])
                completed[0] += 1
            attend(members, not waiting)

    for k in range(steps):
        merge(k)
        if k + 1 < steps:
            place(k + 1)
        if k == 1:
            pl.when(z == 0)(make_names)
        if k >= PASS_LAG:
            pass_on(k - PASS_LAG)
        attend_ready(k - PASS_LAG - DONE_LAG)
    for k in range(max(0, steps - PASS_LAG), steps):
        pass_on(k)
        attend_ready(k - DONE_LAG)
    attend_ready(steps - 1)

    tile = min(COLUMN_TILE, half)
    tiles = half // tile
    loads[5].wait()

    @pl.loop(0, tiles)
    def _(n):
        cols = pl.ds(pl.multiple_of(n * tile, tile), tile)
        part_s[:, cols] = jnp.dot(mine_s[...], own_w[:, cols], preferred_element_type=jnp.float32)

    for c in swaps:
        c.wait_recv()
    for b in range(blocks):
        trade(b).wait_recv()
    gain = jnp.concatenate([gain_s[...]] * (tile // LANES), axis=1)
    for n in range(tiles):
        cols = pl.ds(n * tile, tile)
        summed = part_s[:, cols] + jnp.dot(
            theirs_s[...], got_w[:, cols], preferred_element_type=jnp.float32
        )
        summed = summed.astype(jnp.bfloat16).astype(jnp.float32)
        out_ref[:, cols] = (gain * summed).astype(jnp.bfloat16)

    for c in cnt_copies:
        c.wait_send()
    for far in range(lines - 1):
        pl.when((z >= far) & (z + 1 < lines))(lambda: up_counts(far).wait_send())
    for piece in deals:
        for c in piece:
            c.wait_send()
    for k in range(steps):
        pl.when(z + 1 < lines)(lambda: up(k).wait_send())
        for o in direct:
            across(k, o).wait_send()
        if square:
            for part, peer in ((0, 1), (1, 2)):
                relay(k, part, peer).wait_send()
    for c in swaps:
        c.wait_send()
    for b in range(blocks):
        trade(b).wait_send()


def local(q_home, k_home, value_slots_local, out_weight, router, positions, counts):
    shards = lax.axis_size("ctx")
    lines, plane = arrange(shards)
    sizes = plan(shards)
    steps, room = len(sizes), sum(sizes)
    slots, features = q_home.shape
    keyed = k_home.shape[1]
    width = 2 * keyed
    groups = keyed // HEAD_WIDTH
    share = features // HEAD_WIDTH // groups
    stack = share * QUERY_BLOCK
    blocks = slots // QUERY_BLOCK
    half = out_weight.shape[1] // 2
    deep = max(TILE, QUERY_BLOCK // plane)
    pieces = slots // (deep * plane)
    rows = lambda a: a.reshape(blocks, QUERY_BLOCK)
    vmem, dma = pltpu.VMEM, pltpu.SemaphoreType.DMA
    bf16, f32, i32 = jnp.bfloat16, jnp.float32, jnp.int32
    scratch = [
        vmem((slots, width), bf16),
        vmem((slots, features), bf16),
        vmem((blocks, QUERY_BLOCK), i32),
        vmem((blocks, QUERY_BLOCK), f32),
        vmem((slots, HEAD_WIDTH), f32),
        vmem((slots, HEAD_WIDTH), f32),
        vmem((pieces, plane, deep, width), bf16),
        vmem((pieces, plane, deep, width), bf16),
        vmem((room, width), bf16),
        vmem((plane * room, width), bf16),
        vmem((shards, 8, LANES), i32),
        vmem((plane * room, LANES), i32),
        vmem((blocks, groups, stack, HEAD_WIDTH), bf16),
        vmem((blocks, groups, 1, stack), f32),
        vmem((blocks, groups, 1, stack), f32),
        vmem((blocks, groups, HEAD_WIDTH, stack), f32),
        vmem((slots, LANES), f32),
        vmem((features, half), bf16),
        vmem((features, half), bf16),
        vmem((slots, features), bf16),
        vmem((slots, features), bf16),
        vmem((slots, half), f32),
        dma((6,)),
        dma((2, plane)),
        dma((2, lines)),
        dma((2, pieces, plane)),
        dma((2, steps)),
        dma((2, steps, plane)),
        dma((2, steps, 2)),
        dma((2, SWAP_PARTS)),
        dma((2, blocks)),
    ]
    buffers = [m for m in scratch if m.memory_space == pltpu.VMEM]
    taken = sum(math.prod(m.shape) * jnp.dtype(m.dtype).itemsize for m in buffers)
    placed = lambda a: pltpu.with_memory_space_constraint(a, pltpu.HBM)
    return pl.pallas_call(
        functools.partial(fused_kernel, shards, sizes),
        out_shape=jax.ShapeDtypeStruct((slots, half), bf16),
        in_specs=[pl.BlockSpec(memory_space=pltpu.SMEM)] + [pl.BlockSpec(memory_space=pl.ANY)] * 6,
        out_specs=pl.BlockSpec(memory_space=pltpu.VMEM),
        scratch_shapes=scratch,
        compiler_params=pltpu.CompilerParams(
            collective_id=0, has_side_effects=True, vmem_limit_bytes=taken + SPARE
        ),
        name="fused",
    )(
        counts,
        placed(rows(positions)),
        placed(rows(router)),
        placed(q_home),
        placed(k_home),
        placed(value_slots_local),
        placed(out_weight),
    )


def solution(mesh):
    return jax.shard_map(
        local,
        mesh=mesh,
        in_specs=(
            P("ctx", "head"),
            P("ctx", "head"),
            P("ctx", "head"),
            P("head", None),
            P("ctx"),
            P("ctx"),
            P("ctx"),
        ),
        out_specs=P("ctx", "head"),
        check_vma=False,
    )
```

```python
import functools
import math

import jax
import jax.numpy as jnp
from jax import lax
from jax.experimental import pallas as pl
from jax.experimental.pallas import tpu as pltpu
from jax.sharding import PartitionSpec as P

HEAD_WIDTH = 128
PICKED_PER_SHARD = 128
QUERY_BLOCK = 128
TILE = 16
SWAP_PARTS = 4
LANES = 128
COLUMN_TILE = 512
SPAN = 4
STEP = 48
UNIT_MOST = 768
UNIT_LEAST = 288
ROW_TIME = 0.022
CHAIN_TIME = 0.024
HOP_TIME = 1.7
MERGE_COST = 0.3
UNIT_COST = 0.2
KEY_COST = 0.0016
PASS_LAG = 3
SPARE = 10 << 20
FAR = 1 << 28
LOW = -1e30
QUARTER = 1 << 30
SINE_TERMS = (
    6.283185159611168,
    -41.34165492934356,
    81.60099819261757,
    -76.54965682073457,
    39.53581371237487,
)

rope_theta = 500000.0


def turns_per_position():
    half = HEAD_WIDTH // 2
    turns = [rope_theta ** (-2.0 * i / HEAD_WIDTH) / (2.0 * math.pi) for i in range(half)]
    return [round(t * 4294967296.0) for t in turns]


def cosine_of(phase):
    fold = 0.25 - jnp.abs(phase.astype(jnp.float32) * (1.0 / 4294967296.0))
    square = fold * fold
    total = jnp.full_like(square, SINE_TERMS[-1])
    for term in SINE_TERMS[-2::-1]:
        total = total * square + term
    return total * fold


def turn(x, cosine, sine):
    return x * cosine + pltpu.roll(x, HEAD_WIDTH // 2, 1) * sine


def as_column(row):
    square = jnp.broadcast_to(row, (LANES, LANES))
    return square.T


def arrange(shards):
    side = 1 << ((shards.bit_length() - 1) // 3)
    return shards // (side * side), side * side


def plan(shards):
    lines, plane = arrange(shards)
    most = PICKED_PER_SHARD * lines + lines * (plane - 1) // 2
    room = -(-most // TILE) * TILE
    step = STEP if plane == SPAN else 2 * STEP
    sizes = []
    while sum(sizes) < room:
        grown = TILE << len(sizes) if plane == SPAN else step
        sizes.append(min(grown, step, room - sum(sizes)))
    return tuple(sizes)


def timetable(sizes, blocks):
    steps = len(sizes)
    firsts = [sum(sizes[:i]) for i in range(steps)]
    merge_at = [CHAIN_TIME * (firsts[k] + sizes[k]) for k in range(steps)]
    pass_at, done_at = {}, {}
    events, now, link = [], 0.0, 0.0
    merged = passed = done = 0
    pending = [[] for _ in range(blocks)]

    def owed(b):
        return sum(size for _, _, size in pending[b])

    def attend(b, final=False):
        taken = []
        while pending[b] and (final or sum(t[2] for t in taken) + pending[b][0][2] <= UNIT_MOST):
            taken.append(pending[b].pop(0))
        spans = []
        for o, start, size in sorted(taken):
            if spans and spans[-1][0] == o and spans[-1][1] + spans[-1][2] == start:
                spans[-1][2] += size
            else:
                spans.append([o, start, size])
        events.append(("attend", b, spans, final))
        return UNIT_COST + KEY_COST * sum(t[2] for t in taken)

    def found(o, k):
        for rows in pending:
            rows.append((o, firsts[k], sizes[k]))

    while done < steps:
        if merged < steps and merge_at[merged] <= now:
            events.append(("merge", merged))
            now += MERGE_COST
            link = max(link, now) + ROW_TIME * sizes[merged]
            pass_at[merged] = link + HOP_TIME
            found(0, merged)
            merged += 1
            continue
        if passed in pass_at and pass_at[passed] <= now:
            events.append(("pass", passed))
            link = max(link, now) + ROW_TIME * sizes[passed] / 2
            done_at[passed] = link + HOP_TIME
            found(1, passed)
            found(2, passed)
            passed += 1
            continue
        if done in done_at and done_at[done] <= now:
            events.append(("done", done))
            found(3, done)
            done += 1
            continue
        b = max(range(blocks), key=owed)
        coming = [done_at[done]] if done in done_at else []
        coming += [pass_at[passed]] if passed in pass_at else []
        coming += [merge_at[merged]] if merged < steps else []
        gap = min(coming) - now
        if owed(b) >= UNIT_LEAST or (owed(b) and gap > UNIT_COST + KEY_COST * owed(b)):
            now += attend(b)
        else:
            now += gap
    for b in range(blocks):
        attend(b, True)
    return events


def fused_kernel(
    shards,
    sizes,
    count_ref,
    pos_ref,
    router_ref,
    q_ref,
    k_ref,
    v_ref,
    weight_ref,
    out_ref,
    kin,
    q_in,
    pos_s,
    router_s,
    cos_s,
    sin_s,
    send,
    recv,
    inbox,
    kv,
    cnt_all,
    name_s,
    q_s,
    top_s,
    sum_s,
    acc_s,
    gain_s,
    own_w,
    got_w,
    mine_s,
    theirs_s,
    part_s,
    load_sem,
    cnt_sem,
    up_cnt_sem,
    deal_sem,
    up_sem,
    plane_sem,
    relay_sem,
    swap_sem,
    trade_sem,
    ):
    lines, plane = arrange(shards)
    shift = plane.bit_length() - 1
    me = lax.axis_index("ctx")
    head = lax.axis_index("head")
    other = 1 - head
    z, spot = me // plane, me % plane
    square = plane == 4
    direct = (1, 2) if square else tuple(range(1, plane))
    pieces, _, deep, width = send.shape
    slots = q_in.shape[0]
    span = pieces * plane * deep
    blocks, groups, stack, _ = q_s.shape
    share = stack // QUERY_BLOCK
    keyed = k_ref.shape[1]
    half = own_w.shape[1]
    steps = len(sizes)
    firsts = [sum(sizes[:i]) for i in range(steps)]
    room = sum(sizes)
    factor = 1.4426950408889634 / HEAD_WIDTH**0.5

    count = count_ref[0]
    cnt_all[...] = jnp.zeros_like(cnt_all)
    cnt_all[me] = jnp.full(cnt_all.shape[1:], count, jnp.int32)

    barrier = pltpu.get_barrier_semaphore()
    for o in range(1, plane):
        pl.semaphore_signal(barrier, inc=1, device_id={"ctx": z * plane + (spot ^ o)})
    pl.semaphore_signal(barrier, inc=1, device_id={"head": other})

    @pl.when(z + 1 < lines)
    def _():
        pl.semaphore_signal(barrier, inc=1, device_id={"ctx": me + plane})

    @pl.when(z > 0)
    def _():
        pl.semaphore_signal(barrier, inc=1, device_id={"ctx": me - plane})

    loads = [
        pltpu.make_async_copy(pos_ref, pos_s, load_sem.at[0]),
        pltpu.make_async_copy(k_ref, kin.at[:, pl.ds(0, keyed)], load_sem.at[1]),
        pltpu.make_async_copy(v_ref, kin.at[:, pl.ds(keyed, keyed)], load_sem.at[2]),
        pltpu.make_async_copy(q_ref, q_in, load_sem.at[3]),
        pltpu.make_async_copy(router_ref, router_s, load_sem.at[4]),
        pltpu.make_async_copy(
            weight_ref.at[:, pl.ds(pl.multiple_of(head * half, half), half)],
            own_w,
            load_sem.at[5],
        ),
    ]
    for c in loads[:5]:
        c.start()

    lane = lax.broadcasted_iota(jnp.int32, (1, LANES), 1)
    rate = jnp.zeros((1, LANES), jnp.int32)
    for i, value in enumerate(turns_per_position()):
        rate = jnp.where((lane & (HEAD_WIDTH // 2 - 1)) == i, value, rate)
    lead = jnp.where(lane < HEAD_WIDTH // 2, QUARTER, -QUARTER)
    loads[0].wait()
    for b in range(blocks):
        at = pl.ds(b * QUERY_BLOCK, QUERY_BLOCK)
        column = as_column(pos_s[b : b + 1, :].astype(jnp.float32)).astype(jnp.int32)
        phase = column * rate
        cos_s[at, :] = cosine_of(phase)
        sin_s[at, :] = cosine_of(phase + lead)

    loads[1].wait()
    loads[2].wait()
    block = plane * deep
    row = lax.broadcasted_iota(jnp.int32, (block, block), 0)
    column = lax.broadcasted_iota(jnp.int32, (block, block), 1)
    chosen = column == plane * (row % deep) + row // deep
    deal_map = jnp.where(chosen, 1.0, 0.0).astype(jnp.bfloat16)
    for t in range(pieces):
        at = pl.ds(t * block, block)
        parts = []
        for c in range(keyed // HEAD_WIDTH):
            x = kin[at, pl.ds(c * HEAD_WIDTH, HEAD_WIDTH)].astype(jnp.float32)
            parts.append(turn(x, cos_s[at, :], sin_s[at, :]).astype(jnp.bfloat16))
        parts.append(kin[at, pl.ds(keyed, keyed)])
        rows = jnp.concatenate(parts, axis=1)
        dealt = jnp.dot(deal_map, rows, preferred_element_type=jnp.float32)
        send[t] = dealt.astype(jnp.bfloat16).reshape(plane, deep, width)

    greeted = plane + (z > 0).astype(jnp.int32) + (z + 1 < lines).astype(jnp.int32)
    pl.semaphore_wait(barrier, greeted)

    def mate(o):
        return {"ctx": z * plane + ((spot + o) & (plane - 1))}

    def remote(src, dst, sems, index, target):
        return pltpu.make_async_remote_copy(
            src_ref=src,
            dst_ref=dst,
            send_sem=sems.at[(0,) + index],
            recv_sem=sems.at[(1,) + index],
            device_id=target,
        )

    cnt_copies = [
        remote(cnt_all.at[me], cnt_all.at[me], cnt_sem, (o,), mate(o)) for o in range(1, plane)
    ]
    for c in cnt_copies:
        c.start()
    deals = [
        [
            remote(send.at[t, o], recv.at[t, spot], deal_sem, (t, o), mate(o))
            for o in range(1, plane)
        ]
        for t in range(pieces)
    ]
    for piece in deals:
        for c in piece:
            c.start()
    for t in range(pieces):
        recv[t, spot] = send[t, 0]
    depth = weight_ref.shape[0] // SWAP_PARTS
    columns = pl.ds(pl.multiple_of(other * half, half), half)
    swaps = []
    for i in range(SWAP_PARTS):
        at = pl.ds(i * depth, depth)
        swaps.append(
            remote(
                weight_ref.at[at, columns], got_w.at[at, :], swap_sem, (i,), {"head": other}
            )
        )
    for c in swaps:
        c.start()
    loads[5].start()

    loads[3].wait()

    @pl.loop(0, blocks)
    def _(b):
        top_s[b] = jnp.full_like(top_s[b], LOW)
        sum_s[b] = jnp.zeros_like(sum_s[b])
        acc_s[b] = jnp.zeros_like(acc_s[b])
        at = pl.ds(pl.multiple_of(b * QUERY_BLOCK, QUERY_BLOCK), QUERY_BLOCK)
        cosine, sine = cos_s[at, :] * factor, sin_s[at, :] * factor
        for g in range(groups):
            for h in range(share):
                x = q_in[at, pl.ds((g * share + h) * HEAD_WIDTH, HEAD_WIDTH)].astype(jnp.float32)
                q_s[b, g, pl.ds(h * QUERY_BLOCK, QUERY_BLOCK), :] = turn(x, cosine, sine).astype(
                    jnp.bfloat16
                )

    def table_rows(p):
        return cnt_all.at[pl.ds(p * plane, plane)]

    def up_counts(far):
        rows = table_rows(z - far)
        return remote(rows, rows, up_cnt_sem, (far + 1,), {"ctx": me + plane})

    def up_counts_in(far):
        rows = table_rows(z - far)
        return remote(rows, rows, up_cnt_sem, (far,), {"ctx": me - plane})

    for c in cnt_copies:
        c.wait_recv()
    pl.when(z + 1 < lines)(lambda: up_counts(0).start())
    for far in range(1, lines):

        @pl.when(z >= far)
        def _():
            up_counts_in(far).wait_recv()
            if far + 1 < lines:
                pl.when(z + 1 < lines)(lambda: up_counts(far).start())

    def dealt_to(line, counts, source):
        skip = (line - source) & (plane - 1)
        return (counts + (plane - 1) - skip) >> shift, skip

    counts = cnt_all[:, 0, :]
    shard_row = lax.broadcasted_iota(jnp.int32, counts.shape, 0)
    held, _ = dealt_to(spot, counts, shard_row)
    below = jnp.sum(jnp.where(shard_row < z * plane, held, 0), axis=0, keepdims=True)
    segments = pieces * plane
    seg = lax.broadcasted_iota(jnp.int32, (segments, LANES), 0)
    seg_held = jnp.zeros((segments, LANES), jnp.int32)
    for s in range(plane):
        mine = jnp.broadcast_to(cnt_all[z * plane + s, 0:1, :], seg.shape)
        seg_held = jnp.where((seg & (plane - 1)) == s, mine, seg_held)
    seg_held, _ = dealt_to(spot, seg_held, seg)
    seg_held = jnp.clip(seg_held - deep * (seg >> shift), 0, deep)
    seg_start = jnp.broadcast_to(below, seg.shape)
    for e in range(segments - 1):
        seg_start += jnp.where(seg > e, seg_held[e : e + 1, :], 0)
    wide = (segments, span)
    wide_held = jnp.broadcast_to(seg_held[:, :1], wide)
    wide_start = jnp.broadcast_to(seg_start[:, :1], wide)
    within = lax.broadcasted_iota(jnp.int32, wide, 1) - deep * lax.broadcasted_iota(
        jnp.int32, wide, 0
    )
    live = (within >= 0) & (within < wide_held)
    target = jnp.sum(jnp.where(live, wide_start + within + 1, 0), axis=0, keepdims=True) - 1

    arrived = [0]

    def inner(k):
        return pl.ds(firsts[k], sizes[k])

    def place(k):
        last = firsts[k] + sizes[k]
        needed = min(pieces, -(-last // deep))
        while arrived[0] < needed:
            for c in deals[arrived[0]]:
                c.wait_recv()
            arrived[0] += 1
        used = needed * plane * deep
        spots = lax.broadcasted_iota(jnp.int32, (sizes[k], used), 0) + firsts[k]
        pick = jnp.where(spots == target[:, :used], 1.0, 0.0).astype(jnp.bfloat16)
        rows = recv[pl.ds(0, needed)].reshape(used, width)
        kv[spot, inner(k), :] = jnp.dot(pick, rows, preferred_element_type=jnp.float32).astype(
            jnp.bfloat16
        )

    def up(k):
        return remote(
            kv.at[spot, inner(k), :], inbox.at[inner(k), :], up_sem, (k,), {"ctx": me + plane}
        )

    def up_in(k):
        here = inbox.at[inner(k), :]
        return remote(here, here, up_sem, (k,), {"ctx": me - plane})

    def across(k, o):
        here = kv.at[spot, inner(k), :]
        return remote(here, here, plane_sem, (k, o), {"ctx": z * plane + (spot ^ o)})

    def across_in(k, o):
        here = kv.at[spot ^ o, inner(k), :]
        return remote(here, here, plane_sem, (k, o), {"ctx": z * plane + (spot ^ o)})

    def relay(k, part, peer):
        here = kv.at[spot ^ peer, inner(k), pl.ds(part * keyed, keyed)]
        return remote(
            here, here, relay_sem, (k, part), {"ctx": z * plane + (spot ^ (3 - peer))}
        )

    def relay_in(k, part):
        here = kv.at[spot ^ 3, inner(k), pl.ds(part * keyed, keyed)]
        return remote(here, here, relay_sem, (k, part), {"ctx": z * plane + (spot ^ 3)})

    def merge(k):
        @pl.when(z > 0)
        def _():
            up_in(k).wait_recv()
            kv[spot, inner(k), :] += inbox[inner(k), :]

        @pl.when(z + 1 < lines)
        def _():
            up(k).start()

        for o in direct:
            across(k, o).start()

    def pass_on(k):
        for o in direct:
            across_in(k, o).wait_recv()
        if square:
            for part, peer in ((0, 1), (1, 2)):
                relay(k, part, peer).start()

    def complete(k):
        if square:
            for part in range(2):
                relay_in(k, part).wait_recv()

    ranks = lines * pieces * plane
    lanes = -(-ranks // LANES) * LANES

    def make_names():
        e = lax.broadcasted_iota(jnp.int32, (1, lanes), 1)
        source = e & (plane - 1)
        piece = (e >> shift) & (pieces - 1)
        level = e >> (shift + pieces.bit_length() - 1)
        shard = level * plane + source
        total = jnp.zeros((1, lanes), jnp.int32)
        for d in range(shards):
            number = cnt_all[d, 0:1, :]
            number = jnp.concatenate([number] * (lanes // LANES), axis=1)
            total = jnp.where(shard == d, number, total)
        earlier = jnp.where(
            lax.broadcasted_iota(jnp.int32, (lanes, lanes), 0)
            < lax.broadcasted_iota(jnp.int32, (lanes, lanes), 1),
            1.0,
            0.0,
        ).astype(jnp.bfloat16)

        @pl.loop(0, plane)
        def _(line):
            mine, skip = dealt_to(line, total, source)
            mine = jnp.clip(mine - deep * piece, 0, deep)
            mine = jnp.where(level <= z, mine, 0)
            start = jnp.dot(
                jnp.broadcast_to(mine.astype(jnp.float32), (8, lanes)).astype(jnp.bfloat16),
                earlier,
                preferred_element_type=jnp.float32,
            )[:1].astype(jnp.int32)
            first_name = shard * slots + plane * deep * piece + skip
            within = lax.broadcasted_iota(jnp.int32, (room, lanes), 0) - start
            live = (within >= 0) & (within < mine)
            names = jnp.min(
                jnp.where(live, first_name + plane * within, FAR), axis=1, keepdims=True
            )
            name_s[line] = jnp.broadcast_to(names, (room, LANES))

    def attend(b, pieces_of):
        spots = [(line, pl.ds(start, size)) for line, start, size in pieces_of]
        rows = sum(size for _, _, size in pieces_of)

        def read(ref, cols):
            return jnp.concatenate([ref[line, at, cols] for line, at in spots], axis=0)

        query = me * slots + b * QUERY_BLOCK
        query = query + lax.broadcasted_iota(jnp.int32, (rows, QUERY_BLOCK), 1)
        bias = jnp.where(read(name_s, pl.ds(0, LANES)) <= query, 0.0, LOW)
        bias = jnp.concatenate([bias] * share, axis=1)
        scores = []
        for g in range(groups):
            key = read(kv, pl.ds(g * HEAD_WIDTH, HEAD_WIDTH))
            scores.append(
                lax.dot_general(
                    key, q_s[b, g], (((1,), (1,)), ((), ())), preferred_element_type=jnp.float32
                )
                + bias
            )
        for g in range(groups):
            value = read(kv, pl.ds((groups + g) * HEAD_WIDTH, HEAD_WIDTH))
            value = jnp.concatenate([value, jnp.ones((rows, 8), jnp.bfloat16)], axis=1)
            old = top_s[b, g]
            top = jnp.maximum(old, jnp.max(scores[g], axis=0, keepdims=True))
            terms = jnp.exp2(scores[g] - top).astype(jnp.bfloat16)
            rescale = jnp.exp2(old - top)
            added = lax.dot_general(
                value, terms, (((0,), (0,)), ((), ())), preferred_element_type=jnp.float32
            )
            top_s[b, g] = top
            sum_s[b, g] = sum_s[b, g] * rescale + added[HEAD_WIDTH : HEAD_WIDTH + 1]
            acc_s[b, g] = acc_s[b, g] * rescale + added[:HEAD_WIDTH]

    def block_rows(b):
        return pl.ds(pl.multiple_of(b * QUERY_BLOCK, QUERY_BLOCK), QUERY_BLOCK)

    def trade(b):
        at = block_rows(b)
        return remote(mine_s.at[at, :], theirs_s.at[at, :], trade_sem, (b,), {"head": other})

    def finish(b):
        for g in range(groups):
            done = acc_s[b, g] / sum_s[b, g]
            for h in range(share):
                part = done[:, h * QUERY_BLOCK : (h + 1) * QUERY_BLOCK]
                cols = pl.ds((g * share + h) * HEAD_WIDTH, HEAD_WIDTH)
                mine_s[block_rows(b), cols] = part.T.astype(jnp.bfloat16)
        trade(b).start()

    loads[4].wait()
    for b in range(blocks):
        at = pl.ds(b * QUERY_BLOCK, QUERY_BLOCK)
        live = b * QUERY_BLOCK + lax.broadcasted_iota(jnp.int32, (LANES, LANES), 0) < count
        gain_s[at, :] = jnp.where(live, as_column(router_s[b : b + 1, :]), 0.0)

    place(0)
    pl.when(z > 0)(make_names)

    def step(k):
        merge(k)
        if k + 1 < steps:
            place(k + 1)

    if square:
        named = False
        for kind, at, *rest in timetable(sizes, blocks):
            if kind == "merge":
                step(at)
            elif kind == "pass":
                pass_on(at)
            elif kind == "done":
                complete(at)
            else:
                if not named:
                    pl.when(z == 0)(make_names)
                    named = True
                spans, final = rest
                attend(at, [(spot ^ o, start, size) for o, start, size in spans])
                if final:
                    finish(at)
    else:
        parts = plane // SPAN
        for k in range(steps + PASS_LAG):
            if k < steps:
                step(k)
            at = k - PASS_LAG
            if at < 0:
                continue
            if at == 0:
                pl.when(z == 0)(make_names)
            pass_on(at)

            @pl.loop(0, blocks * parts)
            def _(i):
                b, part = i % blocks, i // blocks
                attend(b, [(part * SPAN + j, firsts[at], sizes[at]) for j in range(SPAN)])
                if at == steps - 1:
                    pl.when(part == parts - 1)(functools.partial(finish, b))

    tile = min(COLUMN_TILE, half)
    tiles = half // tile
    loads[5].wait()

    @pl.loop(0, tiles)
    def _(n):
        cols = pl.ds(pl.multiple_of(n * tile, tile), tile)
        part_s[:, cols] = jnp.dot(mine_s[...], own_w[:, cols], preferred_element_type=jnp.float32)

    for c in swaps:
        c.wait_recv()
    for b in range(blocks):
        trade(b).wait_recv()
    gain = jnp.concatenate([gain_s[...]] * (tile // LANES), axis=1)
    for n in range(tiles):
        cols = pl.ds(n * tile, tile)
        summed = part_s[:, cols] + jnp.dot(
            theirs_s[...], got_w[:, cols], preferred_element_type=jnp.float32
        )
        summed = summed.astype(jnp.bfloat16).astype(jnp.float32)
        out_ref[:, cols] = (gain * summed).astype(jnp.bfloat16)

    for c in cnt_copies:
        c.wait_send()
    for far in range(lines - 1):
        pl.when((z >= far) & (z + 1 < lines))(lambda: up_counts(far).wait_send())
    for piece in deals:
        for c in piece:
            c.wait_send()
    for k in range(steps):
        pl.when(z + 1 < lines)(lambda: up(k).wait_send())
        for o in direct:
            across(k, o).wait_send()
        if square:
            for part, peer in ((0, 1), (1, 2)):
                relay(k, part, peer).wait_send()
    for c in swaps:
        c.wait_send()
    for b in range(blocks):
        trade(b).wait_send()


def local(q_home, k_home, value_slots_local, out_weight, router, positions, counts):
    shards = lax.axis_size("ctx")
    lines, plane = arrange(shards)
    sizes = plan(shards)
    steps, room = len(sizes), sum(sizes)
    slots, features = q_home.shape
    keyed = k_home.shape[1]
    width = 2 * keyed
    groups = keyed // HEAD_WIDTH
    share = features // HEAD_WIDTH // groups
    stack = share * QUERY_BLOCK
    blocks = slots // QUERY_BLOCK
    half = out_weight.shape[1] // 2
    deep = max(TILE, QUERY_BLOCK // plane)
    pieces = slots // (deep * plane)
    rows = lambda a: a.reshape(blocks, QUERY_BLOCK)
    vmem, dma = pltpu.VMEM, pltpu.SemaphoreType.DMA
    bf16, f32, i32 = jnp.bfloat16, jnp.float32, jnp.int32
    scratch = [
        vmem((slots, width), bf16),
        vmem((slots, features), bf16),
        vmem((blocks, QUERY_BLOCK), i32),
        vmem((blocks, QUERY_BLOCK), f32),
        vmem((slots, HEAD_WIDTH), f32),
        vmem((slots, HEAD_WIDTH), f32),
        vmem((pieces, plane, deep, width), bf16),
        vmem((pieces, plane, deep, width), bf16),
        vmem((room, width), bf16),
        vmem((plane, room, width), bf16),
        vmem((shards, 8, LANES), i32),
        vmem((plane, room, LANES), i32),
        vmem((blocks, groups, stack, HEAD_WIDTH), bf16),
        vmem((blocks, groups, 1, stack), f32),
        vmem((blocks, groups, 1, stack), f32),
        vmem((blocks, groups, HEAD_WIDTH, stack), f32),
        vmem((slots, LANES), f32),
        vmem((features, half), bf16),
        vmem((features, half), bf16),
        vmem((slots, features), bf16),
        vmem((slots, features), bf16),
        vmem((slots, half), f32),
        dma((6,)),
        dma((2, plane)),
        dma((2, lines)),
        dma((2, pieces, plane)),
        dma((2, steps)),
        dma((2, steps, plane)),
        dma((2, steps, 2)),
        dma((2, SWAP_PARTS)),
        dma((2, blocks)),
    ]
    buffers = [m for m in scratch if m.memory_space == pltpu.VMEM]
    taken = sum(math.prod(m.shape) * jnp.dtype(m.dtype).itemsize for m in buffers)
    placed = lambda a: pltpu.with_memory_space_constraint(a, pltpu.HBM)
    return pl.pallas_call(
        functools.partial(fused_kernel, shards, sizes),
        out_shape=jax.ShapeDtypeStruct((slots, half), bf16),
        in_specs=[pl.BlockSpec(memory_space=pltpu.SMEM)] + [pl.BlockSpec(memory_space=pl.ANY)] * 6,
        out_specs=pl.BlockSpec(memory_space=pltpu.VMEM),
        scratch_shapes=scratch,
        compiler_params=pltpu.CompilerParams(
            collective_id=0, has_side_effects=True, vmem_limit_bytes=taken + SPARE
        ),
        name="fused",
    )(
        counts,
        placed(rows(positions)),
        placed(rows(router)),
        placed(q_home),
        placed(k_home),
        placed(value_slots_local),
        placed(out_weight),
    )


def solution(mesh):
    return jax.shard_map(
        local,
        mesh=mesh,
        in_specs=(
            P("ctx", "head"),
            P("ctx", "head"),
            P("ctx", "head"),
            P("head", None),
            P("ctx"),
            P("ctx"),
            P("ctx"),
        ),
        out_specs=P("ctx", "head"),
        check_vma=False,
    )
```

```python
import functools
import math

import jax
import jax.numpy as jnp
from jax import lax
from jax.experimental import pallas as pl
from jax.experimental.pallas import tpu as pltpu
from jax.sharding import PartitionSpec as P

HEAD_WIDTH = 128
PICKED_PER_SHARD = 128
QUERY_BLOCK = 128
TILE = 16
SWAP_PARTS = 4
LANES = 128
COLUMN_TILE = 512
SPAN = 4
STEP = 48
UNIT_MOST = 768
UNIT_LEAST = 288
UNIT_SPARE = 96
ROW_TIME = 0.022
CHAIN_TIME = 0.024
HOP_TIME = 1.8
MERGE_COST = 0.3
UNIT_COST = 0.2
KEY_COST = 0.0016
PASS_LAG = 3
SPARE = 10 << 20
FAR = 1 << 28
LOW = -1e30
QUARTER = 1 << 30
SINE_TERMS = (
    6.283185159611168,
    -41.34165492934356,
    81.60099819261757,
    -76.54965682073457,
    39.53581371237487,
)

rope_theta = 500000.0


def turns_per_position():
    half = HEAD_WIDTH // 2
    turns = [rope_theta ** (-2.0 * i / HEAD_WIDTH) / (2.0 * math.pi) for i in range(half)]
    return [round(t * 4294967296.0) for t in turns]


def cosine_of(phase):
    fold = 0.25 - jnp.abs(phase.astype(jnp.float32) * (1.0 / 4294967296.0))
    square = fold * fold
    total = jnp.full_like(square, SINE_TERMS[-1])
    for term in SINE_TERMS[-2::-1]:
        total = total * square + term
    return total * fold


def turn(x, cosine, sine):
    return x * cosine + pltpu.roll(x, HEAD_WIDTH // 2, 1) * sine


def as_column(row):
    square = jnp.broadcast_to(row, (LANES, LANES))
    return square.T


def arrange(shards):
    side = 1 << ((shards.bit_length() - 1) // 3)
    return shards // (side * side), side * side


def plan(shards):
    lines, plane = arrange(shards)
    most = PICKED_PER_SHARD * lines + lines * (plane - 1) // 2
    room = -(-most // TILE) * TILE
    step = STEP if plane == SPAN else 2 * STEP
    sizes = []
    while sum(sizes) < room:
        grown = TILE << len(sizes) if plane == SPAN else step
        sizes.append(min(grown, step, room - sum(sizes)))
    return tuple(sizes)


def timetable(sizes, blocks):
    steps = len(sizes)
    firsts = [sum(sizes[:i]) for i in range(steps)]
    merge_at = [CHAIN_TIME * (firsts[k] + sizes[k]) for k in range(steps)]
    pass_at, done_at = {}, {}
    events, now, link = [], 0.0, 0.0
    merged = passed = done = 0
    pending = [[] for _ in range(blocks)]

    def owed(b):
        return sum(size for _, _, size in pending[b])

    def attend(b, final=False):
        taken = []
        while pending[b] and (final or sum(t[2] for t in taken) + pending[b][0][2] <= UNIT_MOST):
            taken.append(pending[b].pop(0))
        spans = []
        for o, start, size in sorted(taken):
            if spans and spans[-1][0] == o and spans[-1][1] + spans[-1][2] == start:
                spans[-1][2] += size
            else:
                spans.append([o, start, size])
        events.append(("attend", b, spans, final))
        return UNIT_COST + KEY_COST * sum(t[2] for t in taken)

    def found(o, k):
        for rows in pending:
            rows.append((o, firsts[k], sizes[k]))

    while done < steps:
        if merged < steps and merge_at[merged] <= now:
            events.append(("merge", merged))
            now += MERGE_COST
            link = max(link, now) + ROW_TIME * sizes[merged]
            pass_at[merged] = link + HOP_TIME
            found(0, merged)
            merged += 1
            continue
        if passed in pass_at and pass_at[passed] <= now:
            events.append(("pass", passed))
            link = max(link, now) + ROW_TIME * sizes[passed] / 2
            done_at[passed] = link + HOP_TIME
            found(1, passed)
            found(2, passed)
            passed += 1
            continue
        if done in done_at and done_at[done] <= now:
            events.append(("done", done))
            found(3, done)
            done += 1
            continue
        b = max(range(blocks), key=owed)
        coming = [done_at[done]] if done in done_at else []
        coming += [pass_at[passed]] if passed in pass_at else []
        coming += [merge_at[merged]] if merged < steps else []
        gap = min(coming) - now
        spare = gap > UNIT_COST + KEY_COST * owed(b)
        if owed(b) >= UNIT_LEAST or (owed(b) >= UNIT_SPARE and spare):
            now += attend(b)
        else:
            now += gap
    for b in range(blocks):
        attend(b, True)
    return events


def fused_kernel(
    shards,
    sizes,
    count_ref,
    pos_ref,
    router_ref,
    q_ref,
    k_ref,
    v_ref,
    weight_ref,
    out_ref,
    kin,
    q_in,
    pos_s,
    router_s,
    cos_s,
    sin_s,
    send,
    recv,
    inbox,
    kv,
    cnt_all,
    name_s,
    q_s,
    top_s,
    sum_s,
    acc_s,
    gain_s,
    own_w,
    got_w,
    mine_s,
    theirs_s,
    part_s,
    load_sem,
    cnt_sem,
    up_cnt_sem,
    deal_sem,
    up_sem,
    plane_sem,
    relay_sem,
    swap_sem,
    trade_sem,
    ):
    lines, plane = arrange(shards)
    shift = plane.bit_length() - 1
    me = lax.axis_index("ctx")
    head = lax.axis_index("head")
    other = 1 - head
    z, spot = me // plane, me % plane
    square = plane == 4
    direct = (1, 2) if square else tuple(range(1, plane))
    pieces, _, deep, width = send.shape
    slots = q_in.shape[0]
    span = pieces * plane * deep
    blocks, groups, stack, _ = q_s.shape
    share = stack // QUERY_BLOCK
    keyed = k_ref.shape[1]
    half = own_w.shape[1]
    steps = len(sizes)
    firsts = [sum(sizes[:i]) for i in range(steps)]
    room = sum(sizes)
    factor = 1.4426950408889634 / HEAD_WIDTH**0.5

    count = count_ref[0]
    cnt_all[...] = jnp.zeros_like(cnt_all)
    cnt_all[me] = jnp.full(cnt_all.shape[1:], count, jnp.int32)

    barrier = pltpu.get_barrier_semaphore()
    for o in range(1, plane):
        pl.semaphore_signal(barrier, inc=1, device_id={"ctx": z * plane + (spot ^ o)})
    pl.semaphore_signal(barrier, inc=1, device_id={"head": other})

    @pl.when(z + 1 < lines)
    def _():
        pl.semaphore_signal(barrier, inc=1, device_id={"ctx": me + plane})

    @pl.when(z > 0)
    def _():
        pl.semaphore_signal(barrier, inc=1, device_id={"ctx": me - plane})

    loads = [
        pltpu.make_async_copy(pos_ref, pos_s, load_sem.at[0]),
        pltpu.make_async_copy(k_ref, kin.at[:, pl.ds(0, keyed)], load_sem.at[1]),
        pltpu.make_async_copy(v_ref, kin.at[:, pl.ds(keyed, keyed)], load_sem.at[2]),
        pltpu.make_async_copy(q_ref, q_in, load_sem.at[3]),
        pltpu.make_async_copy(router_ref, router_s, load_sem.at[4]),
        pltpu.make_async_copy(
            weight_ref.at[:, pl.ds(pl.multiple_of(head * half, half), half)],
            own_w,
            load_sem.at[5],
        ),
    ]
    for c in loads[:5]:
        c.start()

    lane = lax.broadcasted_iota(jnp.int32, (1, LANES), 1)
    rate = jnp.zeros((1, LANES), jnp.int32)
    for i, value in enumerate(turns_per_position()):
        rate = jnp.where((lane & (HEAD_WIDTH // 2 - 1)) == i, value, rate)
    lead = jnp.where(lane < HEAD_WIDTH // 2, QUARTER, -QUARTER)
    loads[0].wait()
    block = plane * deep
    row = lax.broadcasted_iota(jnp.int32, (block, block), 0)
    column = lax.broadcasted_iota(jnp.int32, (block, block), 1)
    chosen = column == plane * (row % deep) + row // deep
    deal_map = jnp.where(chosen, 1.0, 0.0).astype(jnp.bfloat16)

    def mate(o):
        return {"ctx": z * plane + ((spot + o) & (plane - 1))}

    def remote(src, dst, sems, index, target):
        return pltpu.make_async_remote_copy(
            src_ref=src,
            dst_ref=dst,
            send_sem=sems.at[(0,) + index],
            recv_sem=sems.at[(1,) + index],
            device_id=target,
        )

    cnt_copies = [
        remote(cnt_all.at[me], cnt_all.at[me], cnt_sem, (o,), mate(o)) for o in range(1, plane)
    ]
    deals = [
        [
            remote(send.at[t, o], recv.at[t, spot], deal_sem, (t, o), mate(o))
            for o in range(1, plane)
        ]
        for t in range(pieces)
    ]
    greeted = plane + (z > 0).astype(jnp.int32) + (z + 1 < lines).astype(jnp.int32)
    for t in range(pieces):
        for b in range(t * block // QUERY_BLOCK, (t + 1) * block // QUERY_BLOCK):
            at = pl.ds(b * QUERY_BLOCK, QUERY_BLOCK)
            column = as_column(pos_s[b : b + 1, :].astype(jnp.float32)).astype(jnp.int32)
            phase = column * rate
            cos_s[at, :] = cosine_of(phase)
            sin_s[at, :] = cosine_of(phase + lead)
        if t == 0:
            loads[1].wait()
            loads[2].wait()
        at = pl.ds(t * block, block)
        parts = []
        for c in range(keyed // HEAD_WIDTH):
            x = kin[at, pl.ds(c * HEAD_WIDTH, HEAD_WIDTH)].astype(jnp.float32)
            parts.append(turn(x, cos_s[at, :], sin_s[at, :]).astype(jnp.bfloat16))
        parts.append(kin[at, pl.ds(keyed, keyed)])
        rows = jnp.concatenate(parts, axis=1)
        dealt = jnp.dot(deal_map, rows, preferred_element_type=jnp.float32)
        send[t] = dealt.astype(jnp.bfloat16).reshape(plane, deep, width)
        if t == 0:
            pl.semaphore_wait(barrier, greeted)
            for c in cnt_copies:
                c.start()
        for c in deals[t]:
            c.start()
    for t in range(pieces):
        recv[t, spot] = send[t, 0]
    depth = weight_ref.shape[0] // SWAP_PARTS
    columns = pl.ds(pl.multiple_of(other * half, half), half)
    swaps = []
    for i in range(SWAP_PARTS):
        at = pl.ds(i * depth, depth)
        swaps.append(
            remote(
                weight_ref.at[at, columns], got_w.at[at, :], swap_sem, (i,), {"head": other}
            )
        )
    for c in swaps:
        c.start()
    loads[5].start()

    loads[3].wait()

    @pl.loop(0, blocks)
    def _(b):
        top_s[b] = jnp.full_like(top_s[b], LOW)
        sum_s[b] = jnp.zeros_like(sum_s[b])
        acc_s[b] = jnp.zeros_like(acc_s[b])
        at = pl.ds(pl.multiple_of(b * QUERY_BLOCK, QUERY_BLOCK), QUERY_BLOCK)
        cosine, sine = cos_s[at, :] * factor, sin_s[at, :] * factor
        for g in range(groups):
            for h in range(share):
                x = q_in[at, pl.ds((g * share + h) * HEAD_WIDTH, HEAD_WIDTH)].astype(jnp.float32)
                q_s[b, g, pl.ds(h * QUERY_BLOCK, QUERY_BLOCK), :] = turn(x, cosine, sine).astype(
                    jnp.bfloat16
                )

    def table_rows(p):
        return cnt_all.at[pl.ds(p * plane, plane)]

    def up_counts(far):
        rows = table_rows(z - far)
        return remote(rows, rows, up_cnt_sem, (far + 1,), {"ctx": me + plane})

    def up_counts_in(far):
        rows = table_rows(z - far)
        return remote(rows, rows, up_cnt_sem, (far,), {"ctx": me - plane})

    for c in cnt_copies:
        c.wait_recv()
    pl.when(z + 1 < lines)(lambda: up_counts(0).start())
    for far in range(1, lines):

        @pl.when(z >= far)
        def _():
            up_counts_in(far).wait_recv()
            if far + 1 < lines:
                pl.when(z + 1 < lines)(lambda: up_counts(far).start())

    def dealt_to(line, counts, source):
        skip = (line - source) & (plane - 1)
        return (counts + (plane - 1) - skip) >> shift, skip

    counts = cnt_all[:, 0, :]
    shard_row = lax.broadcasted_iota(jnp.int32, counts.shape, 0)
    held, _ = dealt_to(spot, counts, shard_row)
    below = jnp.sum(jnp.where(shard_row < z * plane, held, 0), axis=0, keepdims=True)
    segments = pieces * plane
    seg = lax.broadcasted_iota(jnp.int32, (segments, LANES), 0)
    seg_held = jnp.zeros((segments, LANES), jnp.int32)
    for s in range(plane):
        mine = jnp.broadcast_to(cnt_all[z * plane + s, 0:1, :], seg.shape)
        seg_held = jnp.where((seg & (plane - 1)) == s, mine, seg_held)
    seg_held, _ = dealt_to(spot, seg_held, seg)
    seg_held = jnp.clip(seg_held - deep * (seg >> shift), 0, deep)
    seg_start = jnp.broadcast_to(below, seg.shape)
    for e in range(segments - 1):
        seg_start += jnp.where(seg > e, seg_held[e : e + 1, :], 0)
    wide = (segments, span)
    wide_held = jnp.broadcast_to(seg_held[:, :1], wide)
    wide_start = jnp.broadcast_to(seg_start[:, :1], wide)
    within = lax.broadcasted_iota(jnp.int32, wide, 1) - deep * lax.broadcasted_iota(
        jnp.int32, wide, 0
    )
    live = (within >= 0) & (within < wide_held)
    target = jnp.sum(jnp.where(live, wide_start + within + 1, 0), axis=0, keepdims=True) - 1

    arrived = [0]

    def inner(k):
        return pl.ds(firsts[k], sizes[k])

    def place(k):
        last = firsts[k] + sizes[k]
        needed = min(pieces, -(-last // deep))
        while arrived[0] < needed:
            for c in deals[arrived[0]]:
                c.wait_recv()
            arrived[0] += 1
        used = needed * plane * deep
        spots = lax.broadcasted_iota(jnp.int32, (sizes[k], used), 0) + firsts[k]
        pick = jnp.where(spots == target[:, :used], 1.0, 0.0).astype(jnp.bfloat16)
        rows = recv[pl.ds(0, needed)].reshape(used, width)
        kv[spot, inner(k), :] = jnp.dot(pick, rows, preferred_element_type=jnp.float32).astype(
            jnp.bfloat16
        )

    def up(k):
        return remote(
            kv.at[spot, inner(k), :], inbox.at[inner(k), :], up_sem, (k,), {"ctx": me + plane}
        )

    def up_in(k):
        here = inbox.at[inner(k), :]
        return remote(here, here, up_sem, (k,), {"ctx": me - plane})

    def across(k, o):
        here = kv.at[spot, inner(k), :]
        return remote(here, here, plane_sem, (k, o), {"ctx": z * plane + (spot ^ o)})

    def across_in(k, o):
        here = kv.at[spot ^ o, inner(k), :]
        return remote(here, here, plane_sem, (k, o), {"ctx": z * plane + (spot ^ o)})

    def relay(k, part, peer):
        here = kv.at[spot ^ peer, inner(k), pl.ds(part * keyed, keyed)]
        return remote(
            here, here, relay_sem, (k, part), {"ctx": z * plane + (spot ^ (3 - peer))}
        )

    def relay_in(k, part):
        here = kv.at[spot ^ 3, inner(k), pl.ds(part * keyed, keyed)]
        return remote(here, here, relay_sem, (k, part), {"ctx": z * plane + (spot ^ 3)})

    def merge(k):
        @pl.when(z > 0)
        def _():
            up_in(k).wait_recv()
            kv[spot, inner(k), :] += inbox[inner(k), :]

        @pl.when(z + 1 < lines)
        def _():
            up(k).start()

        for o in direct:
            across(k, o).start()

    def pass_on(k):
        for o in direct:
            across_in(k, o).wait_recv()
        if square:
            for part, peer in ((0, 1), (1, 2)):
                relay(k, part, peer).start()

    def complete(k):
        if square:
            for part in range(2):
                relay_in(k, part).wait_recv()

    ranks = lines * pieces * plane
    lanes = -(-ranks // LANES) * LANES

    def make_names():
        e = lax.broadcasted_iota(jnp.int32, (1, lanes), 1)
        source = e & (plane - 1)
        piece = (e >> shift) & (pieces - 1)
        level = e >> (shift + pieces.bit_length() - 1)
        shard = level * plane + source
        total = jnp.zeros((1, lanes), jnp.int32)
        for d in range(shards):
            number = cnt_all[d, 0:1, :]
            number = jnp.concatenate([number] * (lanes // LANES), axis=1)
            total = jnp.where(shard == d, number, total)
        earlier = jnp.where(
            lax.broadcasted_iota(jnp.int32, (lanes, lanes), 0)
            < lax.broadcasted_iota(jnp.int32, (lanes, lanes), 1),
            1.0,
            0.0,
        ).astype(jnp.bfloat16)

        @pl.loop(0, plane)
        def _(line):
            mine, skip = dealt_to(line, total, source)
            mine = jnp.clip(mine - deep * piece, 0, deep)
            mine = jnp.where(level <= z, mine, 0)
            start = jnp.dot(
                jnp.broadcast_to(mine.astype(jnp.float32), (8, lanes)).astype(jnp.bfloat16),
                earlier,
                preferred_element_type=jnp.float32,
            )[:1].astype(jnp.int32)
            first_name = shard * slots + plane * deep * piece + skip
            within = lax.broadcasted_iota(jnp.int32, (room, lanes), 0) - start
            live = (within >= 0) & (within < mine)
            names = jnp.min(
                jnp.where(live, first_name + plane * within, FAR), axis=1, keepdims=True
            )
            name_s[line] = jnp.broadcast_to(names, (room, LANES))

    def attend(b, pieces_of):
        spots = [(line, pl.ds(start, size)) for line, start, size in pieces_of]
        rows = sum(size for _, _, size in pieces_of)

        def read(ref, cols):
            return jnp.concatenate([ref[line, at, cols] for line, at in spots], axis=0)

        query = me * slots + b * QUERY_BLOCK
        query = query + lax.broadcasted_iota(jnp.int32, (rows, QUERY_BLOCK), 1)
        bias = jnp.where(read(name_s, pl.ds(0, LANES)) <= query, 0.0, LOW)
        bias = jnp.concatenate([bias] * share, axis=1)
        scores = []
        for g in range(groups):
            key = read(kv, pl.ds(g * HEAD_WIDTH, HEAD_WIDTH))
            scores.append(
                lax.dot_general(
                    key, q_s[b, g], (((1,), (1,)), ((), ())), preferred_element_type=jnp.float32
                )
                + bias
            )
        for g in range(groups):
            value = read(kv, pl.ds((groups + g) * HEAD_WIDTH, HEAD_WIDTH))
            value = jnp.concatenate([value, jnp.ones((rows, 8), jnp.bfloat16)], axis=1)
            old = top_s[b, g]
            top = jnp.maximum(old, jnp.max(scores[g], axis=0, keepdims=True))
            terms = jnp.exp2(scores[g] - top).astype(jnp.bfloat16)
            rescale = jnp.exp2(old - top)
            added = lax.dot_general(
                value, terms, (((0,), (0,)), ((), ())), preferred_element_type=jnp.float32
            )
            top_s[b, g] = top
            sum_s[b, g] = sum_s[b, g] * rescale + added[HEAD_WIDTH : HEAD_WIDTH + 1]
            acc_s[b, g] = acc_s[b, g] * rescale + added[:HEAD_WIDTH]

    def block_rows(b):
        return pl.ds(pl.multiple_of(b * QUERY_BLOCK, QUERY_BLOCK), QUERY_BLOCK)

    def trade(b):
        at = block_rows(b)
        return remote(mine_s.at[at, :], theirs_s.at[at, :], trade_sem, (b,), {"head": other})

    def finish(b):
        for g in range(groups):
            done = acc_s[b, g] / sum_s[b, g]
            for h in range(share):
                part = done[:, h * QUERY_BLOCK : (h + 1) * QUERY_BLOCK]
                cols = pl.ds((g * share + h) * HEAD_WIDTH, HEAD_WIDTH)
                mine_s[block_rows(b), cols] = part.T.astype(jnp.bfloat16)
        trade(b).start()

    loads[4].wait()
    for b in range(blocks):
        at = pl.ds(b * QUERY_BLOCK, QUERY_BLOCK)
        live = b * QUERY_BLOCK + lax.broadcasted_iota(jnp.int32, (LANES, LANES), 0) < count
        gain_s[at, :] = jnp.where(live, as_column(router_s[b : b + 1, :]), 0.0)

    @pl.when(z == 0)
    def _():
        for k in range(steps):
            place(k)
            merge(k)
        make_names()

    arrived[0] = 0

    @pl.when(z > 0)
    def _():
        place(0)
        make_names()

    def step(k):
        @pl.when(z > 0)
        def _():
            merge(k)
            if k + 1 < steps:
                place(k + 1)

    if square:
        for kind, at, *rest in timetable(sizes, blocks):
            if kind == "merge":
                step(at)
            elif kind == "pass":
                pass_on(at)
            elif kind == "done":
                complete(at)
            else:
                spans, final = rest
                attend(at, [(spot ^ o, start, size) for o, start, size in spans])
                if final:
                    finish(at)
    else:
        parts = plane // SPAN
        for k in range(steps + PASS_LAG):
            if k < steps:
                step(k)
            at = k - PASS_LAG
            if at < 0:
                continue
            pass_on(at)

            @pl.loop(0, blocks * parts)
            def _(i):
                b, part = i % blocks, i // blocks
                attend(b, [(part * SPAN + j, firsts[at], sizes[at]) for j in range(SPAN)])
                if at == steps - 1:
                    pl.when(part == parts - 1)(functools.partial(finish, b))

    tile = min(COLUMN_TILE, half)
    tiles = half // tile
    loads[5].wait()

    @pl.loop(0, tiles)
    def _(n):
        cols = pl.ds(pl.multiple_of(n * tile, tile), tile)
        part_s[:, cols] = jnp.dot(mine_s[...], own_w[:, cols], preferred_element_type=jnp.float32)

    for c in swaps:
        c.wait_recv()
    for b in range(blocks):
        trade(b).wait_recv()
    gain = jnp.concatenate([gain_s[...]] * (tile // LANES), axis=1)
    for n in range(tiles):
        cols = pl.ds(n * tile, tile)
        summed = part_s[:, cols] + jnp.dot(
            theirs_s[...], got_w[:, cols], preferred_element_type=jnp.float32
        )
        summed = summed.astype(jnp.bfloat16).astype(jnp.float32)
        out_ref[:, cols] = (gain * summed).astype(jnp.bfloat16)

    for c in cnt_copies:
        c.wait_send()
    for far in range(lines - 1):
        pl.when((z >= far) & (z + 1 < lines))(lambda: up_counts(far).wait_send())
    for piece in deals:
        for c in piece:
            c.wait_send()
    for k in range(steps):
        pl.when(z + 1 < lines)(lambda: up(k).wait_send())
        for o in direct:
            across(k, o).wait_send()
        if square:
            for part, peer in ((0, 1), (1, 2)):
                relay(k, part, peer).wait_send()
    for c in swaps:
        c.wait_send()
    for b in range(blocks):
        trade(b).wait_send()


def local(q_home, k_home, value_slots_local, out_weight, router, positions, counts):
    shards = lax.axis_size("ctx")
    lines, plane = arrange(shards)
    sizes = plan(shards)
    steps, room = len(sizes), sum(sizes)
    slots, features = q_home.shape
    keyed = k_home.shape[1]
    width = 2 * keyed
    groups = keyed // HEAD_WIDTH
    share = features // HEAD_WIDTH // groups
    stack = share * QUERY_BLOCK
    blocks = slots // QUERY_BLOCK
    half = out_weight.shape[1] // 2
    deep = max(TILE, QUERY_BLOCK // plane)
    pieces = slots // (deep * plane)
    rows = lambda a: a.reshape(blocks, QUERY_BLOCK)
    vmem, dma = pltpu.VMEM, pltpu.SemaphoreType.DMA
    bf16, f32, i32 = jnp.bfloat16, jnp.float32, jnp.int32
    scratch = [
        vmem((slots, width), bf16),
        vmem((slots, features), bf16),
        vmem((blocks, QUERY_BLOCK), i32),
        vmem((blocks, QUERY_BLOCK), f32),
        vmem((slots, HEAD_WIDTH), f32),
        vmem((slots, HEAD_WIDTH), f32),
        vmem((pieces, plane, deep, width), bf16),
        vmem((pieces, plane, deep, width), bf16),
        vmem((room, width), bf16),
        vmem((plane, room, width), bf16),
        vmem((shards, 8, LANES), i32),
        vmem((plane, room, LANES), i32),
        vmem((blocks, groups, stack, HEAD_WIDTH), bf16),
        vmem((blocks, groups, 1, stack), f32),
        vmem((blocks, groups, 1, stack), f32),
        vmem((blocks, groups, HEAD_WIDTH, stack), f32),
        vmem((slots, LANES), f32),
        vmem((features, half), bf16),
        vmem((features, half), bf16),
        vmem((slots, features), bf16),
        vmem((slots, features), bf16),
        vmem((slots, half), f32),
        dma((6,)),
        dma((2, plane)),
        dma((2, lines)),
        dma((2, pieces, plane)),
        dma((2, steps)),
        dma((2, steps, plane)),
        dma((2, steps, 2)),
        dma((2, SWAP_PARTS)),
        dma((2, blocks)),
    ]
    buffers = [m for m in scratch if m.memory_space == pltpu.VMEM]
    taken = sum(math.prod(m.shape) * jnp.dtype(m.dtype).itemsize for m in buffers)
    placed = lambda a: pltpu.with_memory_space_constraint(a, pltpu.HBM)
    return pl.pallas_call(
        functools.partial(fused_kernel, shards, sizes),
        out_shape=jax.ShapeDtypeStruct((slots, half), bf16),
        in_specs=[pl.BlockSpec(memory_space=pltpu.SMEM)] + [pl.BlockSpec(memory_space=pl.ANY)] * 6,
        out_specs=pl.BlockSpec(memory_space=pltpu.VMEM),
        scratch_shapes=scratch,
        compiler_params=pltpu.CompilerParams(
            collective_id=0, has_side_effects=True, vmem_limit_bytes=taken + SPARE
        ),
        name="fused",
    )(
        counts,
        placed(rows(positions)),
        placed(rows(router)),
        placed(q_home),
        placed(k_home),
        placed(value_slots_local),
        placed(out_weight),
    )


def solution(mesh):
    return jax.shard_map(
        local,
        mesh=mesh,
        in_specs=(
            P("ctx", "head"),
            P("ctx", "head"),
            P("ctx", "head"),
            P("head", None),
            P("ctx"),
            P("ctx"),
            P("ctx"),
        ),
        out_specs=P("ctx", "head"),
        check_vma=False,
    )
```

```python
import functools
import math

import jax
import jax.numpy as jnp
from jax import lax
from jax.experimental import pallas as pl
from jax.experimental.pallas import tpu as pltpu
from jax.sharding import PartitionSpec as P

HEAD_WIDTH = 128
PICKED_PER_SHARD = 128
QUERY_BLOCK = 128
TILE = 16
SWAP_PARTS = 4
LANES = 128
COLUMN_TILE = 512
SPAN = 4
STEP = 48
UNIT_MOST = 768
UNIT_LEAST = 288
UNIT_SPARE = 96
ROW_TIME = 0.022
CHAIN_TIME = 0.024
HOP_TIME = 1.8
MERGE_COST = 0.3
UNIT_COST = 0.2
KEY_COST = 0.0016
PASS_LAG = 3
ROUTED = 1
SPARE = 10 << 20
FAR = 1 << 28
LOW = -1e30
QUARTER = 1 << 30
SINE_TERMS = (
    6.283185159611168,
    -41.34165492934356,
    81.60099819261757,
    -76.54965682073457,
    39.53581371237487,
)

rope_theta = 500000.0


def turns_per_position():
    half = HEAD_WIDTH // 2
    turns = [rope_theta ** (-2.0 * i / HEAD_WIDTH) / (2.0 * math.pi) for i in range(half)]
    return [round(t * 4294967296.0) for t in turns]


def cosine_of(phase):
    fold = 0.25 - jnp.abs(phase.astype(jnp.float32) * (1.0 / 4294967296.0))
    square = fold * fold
    total = jnp.full_like(square, SINE_TERMS[-1])
    for term in SINE_TERMS[-2::-1]:
        total = total * square + term
    return total * fold


def turn(x, cosine, sine):
    return x * cosine + pltpu.roll(x, HEAD_WIDTH // 2, 1) * sine


def as_column(row):
    square = jnp.broadcast_to(row, (LANES, LANES))
    return square.T


def arrange(shards):
    side = 1 << ((shards.bit_length() - 1) // 3)
    return shards // (side * side), side * side


def plan(shards):
    lines, plane = arrange(shards)
    most = PICKED_PER_SHARD * lines + lines * (plane - 1) // 2
    room = -(-most // TILE) * TILE
    step = STEP if plane == SPAN else 2 * STEP
    sizes = []
    while sum(sizes) < room:
        grown = TILE << len(sizes) if plane == SPAN else step
        sizes.append(min(grown, step, room - sum(sizes)))
    if sizes[-1] > 2 * TILE:
        sizes[-1:] = [sizes[-1] - TILE, TILE]
    return tuple(sizes)


def timetable(sizes, blocks):
    steps = len(sizes)
    firsts = [sum(sizes[:i]) for i in range(steps)]
    merge_at = [CHAIN_TIME * (firsts[k] + sizes[k]) for k in range(steps)]
    pass_at, done_at = {}, {}
    events, now, link = [], 0.0, 0.0
    merged = passed = done = 0
    pending = [[] for _ in range(blocks)]

    def owed(b):
        return sum(size for _, _, size in pending[b])

    def attend(b, final=False):
        taken = []
        while pending[b] and (final or sum(t[2] for t in taken) + pending[b][0][2] <= UNIT_MOST):
            taken.append(pending[b].pop(0))
        spans = []
        for o, start, size in sorted(taken):
            if spans and spans[-1][0] == o and spans[-1][1] + spans[-1][2] == start:
                spans[-1][2] += size
            else:
                spans.append([o, start, size])
        events.append(("attend", b, spans, final))
        return UNIT_COST + KEY_COST * sum(t[2] for t in taken)

    def found(o, k):
        for rows in pending:
            rows.append((o, firsts[k], sizes[k]))

    while done < steps:
        if merged < steps and merge_at[merged] <= now:
            events.append(("merge", merged))
            now += MERGE_COST
            routed = merged >= steps - ROUTED
            link = max(link, now) + ROW_TIME * sizes[merged] * (2 if routed else 1)
            pass_at[merged] = link + HOP_TIME
            found(0, merged)
            merged += 1
            continue
        if passed in pass_at and pass_at[passed] <= now:
            events.append(("pass", passed))
            if passed < steps - ROUTED:
                link = max(link, now) + ROW_TIME * sizes[passed] / 2
                done_at[passed] = link + HOP_TIME
            else:
                done_at[passed] = pass_at[passed] + HOP_TIME / 3
            found(1, passed)
            found(2, passed)
            passed += 1
            continue
        if done in done_at and done_at[done] <= now:
            events.append(("done", done))
            found(3, done)
            done += 1
            continue
        b = max(range(blocks), key=owed)
        coming = [done_at[done]] if done in done_at else []
        coming += [pass_at[passed]] if passed in pass_at else []
        coming += [merge_at[merged]] if merged < steps else []
        gap = min(coming) - now
        spare = gap > UNIT_COST + KEY_COST * owed(b)
        if owed(b) >= UNIT_LEAST or (owed(b) >= UNIT_SPARE and spare):
            now += attend(b)
        else:
            now += gap
    for b in range(blocks):
        attend(b, True)
    return events


def fused_kernel(
    shards,
    sizes,
    count_ref,
    pos_ref,
    router_ref,
    q_ref,
    k_ref,
    v_ref,
    weight_ref,
    out_ref,
    kin,
    q_in,
    pos_s,
    router_s,
    cos_s,
    sin_s,
    send,
    recv,
    inbox,
    kv,
    cnt_all,
    name_s,
    q_s,
    top_s,
    sum_s,
    acc_s,
    gain_s,
    own_w,
    got_w,
    mine_s,
    theirs_s,
    part_s,
    load_sem,
    cnt_sem,
    up_cnt_sem,
    deal_sem,
    up_sem,
    plane_sem,
    relay_sem,
    swap_sem,
    trade_sem,
    ):
    lines, plane = arrange(shards)
    shift = plane.bit_length() - 1
    me = lax.axis_index("ctx")
    head = lax.axis_index("head")
    other = 1 - head
    z, spot = me // plane, me % plane
    square = plane == 4
    direct = (1, 2) if square else tuple(range(1, plane))
    pieces, _, deep, width = send.shape
    slots = q_in.shape[0]
    span = pieces * plane * deep
    blocks, groups, stack, _ = q_s.shape
    share = stack // QUERY_BLOCK
    keyed = k_ref.shape[1]
    half = own_w.shape[1]
    steps = len(sizes)
    firsts = [sum(sizes[:i]) for i in range(steps)]
    room = sum(sizes)
    factor = 1.4426950408889634 / HEAD_WIDTH**0.5

    count = count_ref[0]
    cnt_all[...] = jnp.zeros_like(cnt_all)
    cnt_all[me] = jnp.full(cnt_all.shape[1:], count, jnp.int32)

    barrier = pltpu.get_barrier_semaphore()
    for o in range(1, plane):
        pl.semaphore_signal(barrier, inc=1, device_id={"ctx": z * plane + (spot ^ o)})
    pl.semaphore_signal(barrier, inc=1, device_id={"head": other})

    @pl.when(z + 1 < lines)
    def _():
        pl.semaphore_signal(barrier, inc=1, device_id={"ctx": me + plane})

    @pl.when(z > 0)
    def _():
        pl.semaphore_signal(barrier, inc=1, device_id={"ctx": me - plane})

    loads = [
        pltpu.make_async_copy(pos_ref, pos_s, load_sem.at[0]),
        pltpu.make_async_copy(k_ref, kin.at[:, pl.ds(0, keyed)], load_sem.at[1]),
        pltpu.make_async_copy(v_ref, kin.at[:, pl.ds(keyed, keyed)], load_sem.at[2]),
        pltpu.make_async_copy(q_ref, q_in, load_sem.at[3]),
        pltpu.make_async_copy(router_ref, router_s, load_sem.at[4]),
        pltpu.make_async_copy(
            weight_ref.at[:, pl.ds(pl.multiple_of(head * half, half), half)],
            own_w,
            load_sem.at[5],
        ),
    ]
    for c in loads[:5]:
        c.start()

    lane = lax.broadcasted_iota(jnp.int32, (1, LANES), 1)
    rate = jnp.zeros((1, LANES), jnp.int32)
    for i, value in enumerate(turns_per_position()):
        rate = jnp.where((lane & (HEAD_WIDTH // 2 - 1)) == i, value, rate)
    lead = jnp.where(lane < HEAD_WIDTH // 2, QUARTER, -QUARTER)
    loads[0].wait()
    block = plane * deep
    row = lax.broadcasted_iota(jnp.int32, (block, block), 0)
    column = lax.broadcasted_iota(jnp.int32, (block, block), 1)
    chosen = column == plane * (row % deep) + row // deep
    deal_map = jnp.where(chosen, 1.0, 0.0).astype(jnp.bfloat16)

    def mate(o):
        return {"ctx": z * plane + ((spot + o) & (plane - 1))}

    def remote(src, dst, sems, index, target):
        return pltpu.make_async_remote_copy(
            src_ref=src,
            dst_ref=dst,
            send_sem=sems.at[(0,) + index],
            recv_sem=sems.at[(1,) + index],
            device_id=target,
        )

    cnt_copies = [
        remote(cnt_all.at[me], cnt_all.at[me], cnt_sem, (o,), mate(o)) for o in range(1, plane)
    ]
    deals = [
        [
            remote(send.at[t, o], recv.at[t, spot], deal_sem, (t, o), mate(o))
            for o in range(1, plane)
        ]
        for t in range(pieces)
    ]
    greeted = plane + (z > 0).astype(jnp.int32) + (z + 1 < lines).astype(jnp.int32)
    for t in range(pieces):
        for b in range(t * block // QUERY_BLOCK, (t + 1) * block // QUERY_BLOCK):
            at = pl.ds(b * QUERY_BLOCK, QUERY_BLOCK)
            column = as_column(pos_s[b : b + 1, :].astype(jnp.float32)).astype(jnp.int32)
            phase = column * rate
            cos_s[at, :] = cosine_of(phase)
            sin_s[at, :] = cosine_of(phase + lead)
        if t == 0:
            loads[1].wait()
            loads[2].wait()
        at = pl.ds(t * block, block)
        parts = []
        for c in range(keyed // HEAD_WIDTH):
            x = kin[at, pl.ds(c * HEAD_WIDTH, HEAD_WIDTH)].astype(jnp.float32)
            parts.append(turn(x, cos_s[at, :], sin_s[at, :]).astype(jnp.bfloat16))
        parts.append(kin[at, pl.ds(keyed, keyed)])
        rows = jnp.concatenate(parts, axis=1)
        dealt = jnp.dot(deal_map, rows, preferred_element_type=jnp.float32)
        send[t] = dealt.astype(jnp.bfloat16).reshape(plane, deep, width)
        if t == 0:
            pl.semaphore_wait(barrier, greeted)
            for c in cnt_copies:
                c.start()
        for c in deals[t]:
            c.start()
    for t in range(pieces):
        recv[t, spot] = send[t, 0]
    depth = weight_ref.shape[0] // SWAP_PARTS
    columns = pl.ds(pl.multiple_of(other * half, half), half)
    swaps = []
    for i in range(SWAP_PARTS):
        at = pl.ds(i * depth, depth)
        swaps.append(
            remote(
                weight_ref.at[at, columns], got_w.at[at, :], swap_sem, (i,), {"head": other}
            )
        )

    loads[3].wait()

    @pl.loop(0, blocks)
    def _(b):
        top_s[b] = jnp.full_like(top_s[b], LOW)
        sum_s[b] = jnp.zeros_like(sum_s[b])
        acc_s[b] = jnp.zeros_like(acc_s[b])
        at = pl.ds(pl.multiple_of(b * QUERY_BLOCK, QUERY_BLOCK), QUERY_BLOCK)
        cosine, sine = cos_s[at, :] * factor, sin_s[at, :] * factor
        for g in range(groups):
            for h in range(share):
                x = q_in[at, pl.ds((g * share + h) * HEAD_WIDTH, HEAD_WIDTH)].astype(jnp.float32)
                q_s[b, g, pl.ds(h * QUERY_BLOCK, QUERY_BLOCK), :] = turn(x, cosine, sine).astype(
                    jnp.bfloat16
                )

    def table_rows(p):
        return cnt_all.at[pl.ds(p * plane, plane)]

    def up_counts(far):
        rows = table_rows(z - far)
        return remote(rows, rows, up_cnt_sem, (far + 1,), {"ctx": me + plane})

    def up_counts_in(far):
        rows = table_rows(z - far)
        return remote(rows, rows, up_cnt_sem, (far,), {"ctx": me - plane})

    for c in cnt_copies:
        c.wait_recv()
    pl.when(z + 1 < lines)(lambda: up_counts(0).start())
    for far in range(1, lines):

        @pl.when(z >= far)
        def _():
            up_counts_in(far).wait_recv()
            if far + 1 < lines:
                pl.when(z + 1 < lines)(lambda: up_counts(far).start())

    def dealt_to(line, counts, source):
        skip = (line - source) & (plane - 1)
        return (counts + (plane - 1) - skip) >> shift, skip

    counts = cnt_all[:, 0, :]
    shard_row = lax.broadcasted_iota(jnp.int32, counts.shape, 0)
    held, _ = dealt_to(spot, counts, shard_row)
    below = jnp.sum(jnp.where(shard_row < z * plane, held, 0), axis=0, keepdims=True)
    segments = pieces * plane
    seg = lax.broadcasted_iota(jnp.int32, (segments, LANES), 0)
    seg_held = jnp.zeros((segments, LANES), jnp.int32)
    for s in range(plane):
        mine = jnp.broadcast_to(cnt_all[z * plane + s, 0:1, :], seg.shape)
        seg_held = jnp.where((seg & (plane - 1)) == s, mine, seg_held)
    seg_held, _ = dealt_to(spot, seg_held, seg)
    seg_held = jnp.clip(seg_held - deep * (seg >> shift), 0, deep)
    seg_start = jnp.broadcast_to(below, seg.shape)
    for e in range(segments - 1):
        seg_start += jnp.where(seg > e, seg_held[e : e + 1, :], 0)
    wide = (segments, span)
    wide_held = jnp.broadcast_to(seg_held[:, :1], wide)
    wide_start = jnp.broadcast_to(seg_start[:, :1], wide)
    within = lax.broadcasted_iota(jnp.int32, wide, 1) - deep * lax.broadcasted_iota(
        jnp.int32, wide, 0
    )
    live = (within >= 0) & (within < wide_held)
    target = jnp.sum(jnp.where(live, wide_start + within + 1, 0), axis=0, keepdims=True) - 1

    arrived = [0]

    def inner(k):
        return pl.ds(firsts[k], sizes[k])

    def place(k):
        last = firsts[k] + sizes[k]
        needed = min(pieces, -(-last // deep))
        while arrived[0] < needed:
            for c in deals[arrived[0]]:
                c.wait_recv()
            arrived[0] += 1
        used = needed * plane * deep
        spots = lax.broadcasted_iota(jnp.int32, (sizes[k], used), 0) + firsts[k]
        pick = jnp.where(spots == target[:, :used], 1.0, 0.0).astype(jnp.bfloat16)
        rows = recv[pl.ds(0, needed)].reshape(used, width)
        kv[spot, inner(k), :] = jnp.dot(pick, rows, preferred_element_type=jnp.float32).astype(
            jnp.bfloat16
        )

    def up(k):
        return remote(
            kv.at[spot, inner(k), :], inbox.at[inner(k), :], up_sem, (k,), {"ctx": me + plane}
        )

    def up_in(k):
        here = inbox.at[inner(k), :]
        return remote(here, here, up_sem, (k,), {"ctx": me - plane})

    def across(k, o):
        here = kv.at[spot, inner(k), :]
        return remote(here, here, plane_sem, (k, o), {"ctx": z * plane + (spot ^ o)})

    def across_in(k, o):
        here = kv.at[spot ^ o, inner(k), :]
        return remote(here, here, plane_sem, (k, o), {"ctx": z * plane + (spot ^ o)})

    def relay(k, part, peer):
        here = kv.at[spot ^ peer, inner(k), pl.ds(part * keyed, keyed)]
        return remote(
            here, here, relay_sem, (k, part), {"ctx": z * plane + (spot ^ (3 - peer))}
        )

    def relay_in(k, part):
        here = kv.at[spot ^ 3, inner(k), pl.ds(part * keyed, keyed)]
        return remote(here, here, relay_sem, (k, part), {"ctx": z * plane + (spot ^ 3)})

    def relayed(k):
        return square and k < steps - ROUTED

    def sent_to(k):
        return direct if relayed(k) or not square else (3,) + direct

    def merge(k):
        @pl.when(z > 0)
        def _():
            up_in(k).wait_recv()
            kv[spot, inner(k), :] += inbox[inner(k), :]

        @pl.when(z + 1 < lines)
        def _():
            up(k).start()

        for o in sent_to(k):
            across(k, o).start()

    def pass_on(k):
        for o in direct:
            across_in(k, o).wait_recv()
        if relayed(k):
            for part, peer in ((0, 1), (1, 2)):
                relay(k, part, peer).start()

    def complete(k):
        if relayed(k):
            for part in range(2):
                relay_in(k, part).wait_recv()
        elif square:
            across_in(k, 3).wait_recv()

    ranks = lines * pieces * plane
    lanes = -(-ranks // LANES) * LANES

    def make_names():
        e = lax.broadcasted_iota(jnp.int32, (1, lanes), 1)
        source = e & (plane - 1)
        piece = (e >> shift) & (pieces - 1)
        level = e >> (shift + pieces.bit_length() - 1)
        shard = level * plane + source
        total = jnp.zeros((1, lanes), jnp.int32)
        for d in range(shards):
            number = cnt_all[d, 0:1, :]
            number = jnp.concatenate([number] * (lanes // LANES), axis=1)
            total = jnp.where(shard == d, number, total)
        earlier = jnp.where(
            lax.broadcasted_iota(jnp.int32, (lanes, lanes), 0)
            < lax.broadcasted_iota(jnp.int32, (lanes, lanes), 1),
            1.0,
            0.0,
        ).astype(jnp.bfloat16)

        @pl.loop(0, plane)
        def _(line):
            mine, skip = dealt_to(line, total, source)
            mine = jnp.clip(mine - deep * piece, 0, deep)
            mine = jnp.where(level <= z, mine, 0)
            start = jnp.dot(
                jnp.broadcast_to(mine.astype(jnp.float32), (8, lanes)).astype(jnp.bfloat16),
                earlier,
                preferred_element_type=jnp.float32,
            )[:1].astype(jnp.int32)
            first_name = shard * slots + plane * deep * piece + skip
            within = lax.broadcasted_iota(jnp.int32, (room, lanes), 0) - start
            live = (within >= 0) & (within < mine)
            names = jnp.min(
                jnp.where(live, first_name + plane * within, FAR), axis=1, keepdims=True
            )
            name_s[line] = jnp.broadcast_to(names, (room, LANES))

    def attend(b, pieces_of):
        spots = [(line, pl.ds(start, size)) for line, start, size in pieces_of]
        rows = sum(size for _, _, size in pieces_of)

        def read(ref, cols):
            return jnp.concatenate([ref[line, at, cols] for line, at in spots], axis=0)

        query = me * slots + b * QUERY_BLOCK
        query = query + lax.broadcasted_iota(jnp.int32, (rows, QUERY_BLOCK), 1)
        bias = jnp.where(read(name_s, pl.ds(0, LANES)) <= query, 0.0, LOW)
        bias = jnp.concatenate([bias] * share, axis=1)
        scores = []
        for g in range(groups):
            key = read(kv, pl.ds(g * HEAD_WIDTH, HEAD_WIDTH))
            scores.append(
                lax.dot_general(
                    key, q_s[b, g], (((1,), (1,)), ((), ())), preferred_element_type=jnp.float32
                )
                + bias
            )
        for g in range(groups):
            value = read(kv, pl.ds((groups + g) * HEAD_WIDTH, HEAD_WIDTH))
            value = jnp.concatenate([value, jnp.ones((rows, 8), jnp.bfloat16)], axis=1)
            old = top_s[b, g]
            top = jnp.maximum(old, jnp.max(scores[g], axis=0, keepdims=True))
            terms = jnp.exp2(scores[g] - top).astype(jnp.bfloat16)
            rescale = jnp.exp2(old - top)
            added = lax.dot_general(
                value, terms, (((0,), (0,)), ((), ())), preferred_element_type=jnp.float32
            )
            top_s[b, g] = top
            sum_s[b, g] = sum_s[b, g] * rescale + added[HEAD_WIDTH : HEAD_WIDTH + 1]
            acc_s[b, g] = acc_s[b, g] * rescale + added[:HEAD_WIDTH]

    def block_rows(b):
        return pl.ds(pl.multiple_of(b * QUERY_BLOCK, QUERY_BLOCK), QUERY_BLOCK)

    def trade(b):
        at = block_rows(b)
        return remote(mine_s.at[at, :], theirs_s.at[at, :], trade_sem, (b,), {"head": other})

    def finish(b):
        for g in range(groups):
            done = acc_s[b, g] / sum_s[b, g]
            for h in range(share):
                part = done[:, h * QUERY_BLOCK : (h + 1) * QUERY_BLOCK]
                cols = pl.ds((g * share + h) * HEAD_WIDTH, HEAD_WIDTH)
                mine_s[block_rows(b), cols] = part.T.astype(jnp.bfloat16)
        trade(b).start()

    loads[4].wait()
    for b in range(blocks):
        at = pl.ds(b * QUERY_BLOCK, QUERY_BLOCK)
        live = b * QUERY_BLOCK + lax.broadcasted_iota(jnp.int32, (LANES, LANES), 0) < count
        gain_s[at, :] = jnp.where(live, as_column(router_s[b : b + 1, :]), 0.0)

    @pl.when(z == 0)
    def _():
        for k in range(steps):
            place(k)
            merge(k)
        make_names()

    arrived[0] = 0

    @pl.when(z > 0)
    def _():
        place(0)
        make_names()

    def step(k):
        @pl.when(z > 0)
        def _():
            merge(k)
            if k + 1 < steps:
                place(k + 1)

    if square:
        for kind, at, *rest in timetable(sizes, blocks):
            if kind == "merge":
                step(at)
                if at == 3:
                    for c in swaps:
                        c.start()
                    loads[5].start()
            elif kind == "pass":
                pass_on(at)
            elif kind == "done":
                complete(at)
            else:
                spans, final = rest
                attend(at, [(spot ^ o, start, size) for o, start, size in spans])
                if final:
                    finish(at)
    else:
        parts = plane // SPAN
        for c in swaps:
            c.start()
        loads[5].start()
        for k in range(steps + PASS_LAG):
            if k < steps:
                step(k)
            at = k - PASS_LAG
            if at < 0:
                continue
            pass_on(at)

            @pl.loop(0, blocks * parts)
            def _(i):
                b, part = i % blocks, i // blocks
                attend(b, [(part * SPAN + j, firsts[at], sizes[at]) for j in range(SPAN)])
                if at == steps - 1:
                    pl.when(part == parts - 1)(functools.partial(finish, b))

    tile = min(COLUMN_TILE, half)
    tiles = half // tile
    loads[5].wait()

    @pl.loop(0, tiles)
    def _(n):
        cols = pl.ds(pl.multiple_of(n * tile, tile), tile)
        part_s[:, cols] = jnp.dot(mine_s[...], own_w[:, cols], preferred_element_type=jnp.float32)

    for c in swaps:
        c.wait_recv()
    for b in range(blocks):
        trade(b).wait_recv()
    gain = jnp.concatenate([gain_s[...]] * (tile // LANES), axis=1)
    for n in range(tiles):
        cols = pl.ds(n * tile, tile)
        summed = part_s[:, cols] + jnp.dot(
            theirs_s[...], got_w[:, cols], preferred_element_type=jnp.float32
        )
        summed = summed.astype(jnp.bfloat16).astype(jnp.float32)
        out_ref[:, cols] = (gain * summed).astype(jnp.bfloat16)

    for c in cnt_copies:
        c.wait_send()
    for far in range(lines - 1):
        pl.when((z >= far) & (z + 1 < lines))(lambda: up_counts(far).wait_send())
    for piece in deals:
        for c in piece:
            c.wait_send()
    for k in range(steps):
        pl.when(z + 1 < lines)(lambda: up(k).wait_send())
        for o in sent_to(k):
            across(k, o).wait_send()
        if relayed(k):
            for part, peer in ((0, 1), (1, 2)):
                relay(k, part, peer).wait_send()
    for c in swaps:
        c.wait_send()
    for b in range(blocks):
        trade(b).wait_send()


def local(q_home, k_home, value_slots_local, out_weight, router, positions, counts):
    shards = lax.axis_size("ctx")
    lines, plane = arrange(shards)
    sizes = plan(shards)
    steps, room = len(sizes), sum(sizes)
    slots, features = q_home.shape
    keyed = k_home.shape[1]
    width = 2 * keyed
    groups = keyed // HEAD_WIDTH
    share = features // HEAD_WIDTH // groups
    stack = share * QUERY_BLOCK
    blocks = slots // QUERY_BLOCK
    half = out_weight.shape[1] // 2
    deep = max(TILE, QUERY_BLOCK // plane)
    pieces = slots // (deep * plane)
    rows = lambda a: a.reshape(blocks, QUERY_BLOCK)
    vmem, dma = pltpu.VMEM, pltpu.SemaphoreType.DMA
    bf16, f32, i32 = jnp.bfloat16, jnp.float32, jnp.int32
    scratch = [
        vmem((slots, width), bf16),
        vmem((slots, features), bf16),
        vmem((blocks, QUERY_BLOCK), i32),
        vmem((blocks, QUERY_BLOCK), f32),
        vmem((slots, HEAD_WIDTH), f32),
        vmem((slots, HEAD_WIDTH), f32),
        vmem((pieces, plane, deep, width), bf16),
        vmem((pieces, plane, deep, width), bf16),
        vmem((room, width), bf16),
        vmem((plane, room, width), bf16),
        vmem((shards, 8, LANES), i32),
        vmem((plane, room, LANES), i32),
        vmem((blocks, groups, stack, HEAD_WIDTH), bf16),
        vmem((blocks, groups, 1, stack), f32),
        vmem((blocks, groups, 1, stack), f32),
        vmem((blocks, groups, HEAD_WIDTH, stack), f32),
        vmem((slots, LANES), f32),
        vmem((features, half), bf16),
        vmem((features, half), bf16),
        vmem((slots, features), bf16),
        vmem((slots, features), bf16),
        vmem((slots, half), f32),
        dma((6,)),
        dma((2, plane)),
        dma((2, lines)),
        dma((2, pieces, plane)),
        dma((2, steps)),
        dma((2, steps, plane)),
        dma((2, steps, 2)),
        dma((2, SWAP_PARTS)),
        dma((2, blocks)),
    ]
    buffers = [m for m in scratch if m.memory_space == pltpu.VMEM]
    taken = sum(math.prod(m.shape) * jnp.dtype(m.dtype).itemsize for m in buffers)
    placed = lambda a: pltpu.with_memory_space_constraint(a, pltpu.HBM)
    return pl.pallas_call(
        functools.partial(fused_kernel, shards, sizes),
        out_shape=jax.ShapeDtypeStruct((slots, half), bf16),
        in_specs=[pl.BlockSpec(memory_space=pltpu.SMEM)] + [pl.BlockSpec(memory_space=pl.ANY)] * 6,
        out_specs=pl.BlockSpec(memory_space=pltpu.VMEM),
        scratch_shapes=scratch,
        compiler_params=pltpu.CompilerParams(
            collective_id=0, has_side_effects=True, vmem_limit_bytes=taken + SPARE
        ),
        name="fused",
    )(
        counts,
        placed(rows(positions)),
        placed(rows(router)),
        placed(q_home),
        placed(k_home),
        placed(value_slots_local),
        placed(out_weight),
    )


def solution(mesh):
    return jax.shard_map(
        local,
        mesh=mesh,
        in_specs=(
            P("ctx", "head"),
            P("ctx", "head"),
            P("ctx", "head"),
            P("head", None),
            P("ctx"),
            P("ctx"),
            P("ctx"),
        ),
        out_specs=P("ctx", "head"),
        check_vma=False,
    )
```
